256 devices in a mesh: rows: 64 (over x_hi, z, y), cols: 4 (over x_lo, core).
Axes of the slice: x: 4 (x_hi: 2, x_lo: 2; x = x_hi * 2 + x_lo), y: 4, z: 8, core: 2. Of those that a mesh axis runs over, the one named last changes fastest.
Arguments:
- features: bfloat16 [65536, 1024], P('rows', 'cols'), may hold values from -6 to 6
- targets: float32 [65536, 2048], P('rows', 'cols'), may hold values from -6 to 6
- block_index: int32 [2, 512], replicated, may hold values from 0 to 65535, as said below
Outputs:
- coefs: float32 [65536, 2048], P('rows', 'cols')
- residual: float32 [65536, 2048], P('rows', 'cols')
The draws below stay inside these ranges and needn't reach their ends.
Inputs may be any that keep to these rules, and one draw needn't show every extreme that they name: `block_index`: the 2 x 512 indices are all distinct.
All inputs are finite; a program needn't handle non-finite values.
Results may differ from the reference program's by a relative error of at most 0.0003.
Values may be sent and summed in bfloat16 or wider, within the bound.
No kernel may reach another device: no remote copies, remote signals or barrier semaphores. Data moves between devices by JAX's collectives and lax.ppermute only.
A program may use at most 64 MiB of HBM per device.

```python
import jax
import jax.numpy as jnp
from jax import lax

D_IN = 1024
TGT = 2048
BLOCK = 512
STEPS = 2
ROWS = 65536


latent_width = 8


project_scale = 0.17


noise_scale = 0.2


def draw_features(key, part):
    latent_key = jax.random.fold_in(key, 11)
    scale_key = jax.random.fold_in(key, 12)
    project_key = jax.random.fold_in(key, 13)
    noise_key = jax.random.fold_in(key, 14)
    latent = jax.random.normal(latent_key, (ROWS, latent_width), jnp.float32)
    scales = jnp.exp(jax.random.uniform(scale_key, (latent_width,), jnp.float32, jnp.log(0.4), jnp.log(2.5)))
    project = project_scale * jax.random.normal(project_key, (latent_width, D_IN), jnp.float32)
    noise = noise_scale * jax.random.normal(noise_key, (ROWS, D_IN), jnp.float32)
    values = jnp.dot(latent * scales[None, :], project, precision=lax.Precision.HIGHEST) + noise
    return jnp.clip(values, -6.0, 6.0).astype(jnp.bfloat16)


def draw_block_index(key, part):
    order = jax.random.permutation(jax.random.fold_in(key, 7), ROWS)
    return order[:STEPS * BLOCK].reshape(STEPS, BLOCK).astype(jnp.int32)


def block_levels(own_key, dims, shards, smallest, top_value):
    gain, own = 1.0, jax.random.fold_in(own_key, 6)
    for dim, shards_of in shards:
        heights = jnp.exp(jax.random.uniform(jax.random.fold_in(own, dim), (shards_of,), jnp.float32, smallest / len(shards), top_value / len(shards)))
        gain = gain * jnp.repeat(heights, dims[dim] // shards_of).reshape([-1 if axis == dim else 1 for axis in range(len(dims))])
    return gain


def scatter_about(own_key, extent, scale, reach, shards=(), kind=jnp.bfloat16):
    array = jax.random.normal(own_key, extent, jnp.float32) * scale
    if len(shards) > 0:
        array = block_levels(own_key, extent, shards, -0.22, 0.18) * array
    return jnp.clip(array, min=-reach, max=reach).astype(kind)


def setup_inputs(seed: int = 0) -> dict:
    arg_keys = jax.random.split(jax.random.key(seed), 4)
    features = draw_features(jax.random.fold_in(arg_keys[3], 71), 0)
    targets = scatter_about(arg_keys[1], (ROWS, TGT), 1.0, 6.0, ((0, 64), (1, 4)), jnp.float32)
    block_index = draw_block_index(jax.random.fold_in(arg_keys[3], 71), 0)
    return {"features": features, "targets": targets, "block_index": block_index}


ridge_value = 1.0

def kernel(left, right):
    gram = jnp.dot(left.astype(jnp.float32), right.T.astype(jnp.float32), preferred_element_type=jnp.float32)
    left_sq = jnp.sum(jnp.square(left.astype(jnp.float32)), axis=1)
    right_sq = jnp.sum(jnp.square(right.astype(jnp.float32)), axis=1)
    return jnp.exp(-(2.0 / D_IN) * (left_sq[:, None] + right_sq[None, :] - 2.0 * gram))

def reference(features, targets, block_index):
    coefs = jnp.zeros(targets.shape, jnp.float32)
    residual = targets
    for step in range(STEPS):
        chosen = block_index[step].astype(jnp.int32)
        points = features[chosen]
        picked = residual[chosen]
        slab = kernel(features, points)
        inner = kernel(points, points)
        system = inner + ridge_value * jnp.eye(BLOCK, dtype=jnp.float32)
        factor = jnp.linalg.cholesky(system)
        delta = jax.scipy.linalg.cho_solve((factor, True), picked)
        coefs = coefs.at[chosen].add(delta)
        residual = residual - jnp.dot(slab, delta, precision=lax.Precision.HIGHEST)
        residual = residual.at[chosen].add(-ridge_value * delta)
    return (coefs, residual)
```

```python
import functools

import jax
import jax.numpy as jnp
from jax import lax
from jax.experimental import pallas as pl
from jax.experimental.pallas import tpu as pltpu
from jax.sharding import Mesh
from jax.sharding import PartitionSpec as P

ROWS = ("r0", "r1", "r2")
COLS = ("xlo", "core")
RIDGE = 1.0
LEAF = 128
HI = lax.Precision.HIGHEST
SWAP = [(0, 1), (1, 0)]


def mm(a, b):
    return lax.dot_general(a, b, (((1,), (0,)), ((), ())), precision=HI, preferred_element_type=jnp.float32)


def mm_nt(a, b):
    return lax.dot_general(a, b, (((1,), (1,)), ((), ())), preferred_element_type=jnp.float32)


def inv2(a, b, d):
    i = 1.0 / (a * d - b * b)
    return d * i, -b * i, a * i


def leaf_inverse(m):
    n = m.shape[-1]
    lane = lax.broadcasted_iota(jnp.int32, (1, 1, n), 2)
    sub = lax.broadcasted_iota(jnp.int32, (1, n, 1), 1)
    for j in range(0, n, 4):
        c = [jnp.broadcast_to(m[:, :, j + q : j + q + 1], m.shape) for q in range(4)]
        e = lambda p, q: c[q][:, j + p : j + p + 1, :]
        r = []
        for q in range(4):
            row = m[:, j + q : j + q + 1, :]
            for w in range(4):
                row = jnp.where(lane == j + w, 1.0 if w == q else 0.0, row)
            r.append(row)
        x11, x12, x22 = inv2(e(0, 0), e(0, 1), e(1, 1))
        b = [[e(0, 2), e(0, 3)], [e(1, 2), e(1, 3)]]
        y = [
            [x11 * b[0][q] + x12 * b[1][q] for q in range(2)],
            [x12 * b[0][q] + x22 * b[1][q] for q in range(2)],
        ]
        s = lambda p, q, base: base - (b[0][p] * y[0][q] + b[1][p] * y[1][q])
        z11, z12, z22 = inv2(s(0, 0, e(2, 2)), s(0, 1, e(2, 3)), s(1, 1, e(3, 3)))
        w0 = x11 * r[0] + x12 * r[1]
        w1 = x12 * r[0] + x22 * r[1]
        t0 = r[2] - (b[0][0] * w0 + b[1][0] * w1)
        t1 = r[3] - (b[0][1] * w0 + b[1][1] * w1)
        s2 = z11 * t0 + z12 * t1
        s3 = z12 * t0 + z22 * t1
        s0 = w0 - (y[0][0] * s2 + y[0][1] * s3)
        s1 = w1 - (y[1][0] * s2 + y[1][1] * s3)
        new = jnp.where((lane >= j) & (lane < j + 4), 0.0, m)
        new = new - ((c[0] * s0 + c[1] * s1) + (c[2] * s2 + c[3] * s3))
        for q, sq in enumerate((s0, s1, s2, s3)):
            new = jnp.where(sub == j + q, sq, new)
        m = new
    return m


def pick_points_kernel(idx_ref, f_ref, o_ref):
    n = f_ref.shape[0]
    sel = (idx_ref[...] == lax.broadcasted_iota(jnp.int32, (idx_ref.shape[0], n), 1)).astype(jnp.bfloat16)
    o_ref[...] = jnp.dot(sel, f_ref[...], preferred_element_type=jnp.float32).astype(jnp.bfloat16)


def split3(x):
    hi = x.astype(jnp.bfloat16)
    rest = x - hi.astype(jnp.float32)
    mid = rest.astype(jnp.bfloat16)
    low = (rest - mid.astype(jnp.float32)).astype(jnp.bfloat16)
    return hi, mid, low


def pick_targets_kernel(idx_ref, t_ref, o_ref, parts):
    n, w = t_ref.shape

    @pl.when(pl.program_id(0) == 0)
    def _():
        for i, part in enumerate(split3(t_ref[...])):
            parts[:, i * w : (i + 1) * w] = part

    sel = (idx_ref[...] == lax.broadcasted_iota(jnp.int32, (idx_ref.shape[0], n), 1)).astype(jnp.bfloat16)
    got = jnp.dot(sel, parts[...], preferred_element_type=jnp.float32)
    o_ref[...] = (got[:, :w] + got[:, w : 2 * w]) + got[:, 2 * w :]


def factor_kernel(p0, p1, p2, p3, w_ref, pn_ref, a_ref, r_ref, *, width):
    points = (p0, p1, p2, p3)
    n = p0.shape[0] // 2
    gram = lambda a, b: sum(mm_nt(p[a * n : (a + 1) * n, :], p[b * n : (b + 1) * n, :]) for p in points)
    eye = lax.broadcasted_iota(jnp.int32, (n, n), 0) == lax.broadcasted_iota(jnp.int32, (n, n), 1)
    scale = -(2.0 / width)
    rows, cols = [], []
    for s in range(2):
        g = gram(s, s)
        diag = jnp.where(eye, g, 0.0)
        rows.append(jnp.sum(diag, axis=0, keepdims=True))
        cols.append(jnp.sum(diag, axis=1, keepdims=True))
        k = jnp.exp(scale * (cols[s] + rows[s] - 2.0 * g))
        a_ref[s] = k + jnp.where(eye, RIDGE, 0.0)
        pn_ref[:, s * n : (s + 1) * n] = jnp.broadcast_to(rows[s], (8, n))
    w_ref[n:, :n] = jnp.exp(scale * (cols[1] + rows[0] - 2.0 * gram(1, 0)))
    w_ref[:n, n:] = jnp.zeros((n, n), jnp.float32)

    def step(k, carry):
        at = pl.ds(pl.multiple_of(k * LEAF, LEAF), LEAF)
        dinv = leaf_inverse(a_ref[:, at, at])
        for s in range(2):
            r_ref[s] = mm(dinv[s], a_ref[s, at, :])
            r_ref[s, :, at] = dinv[s]
            col = a_ref[s, :, at]
            a_ref[s, :, at] = jnp.zeros((n, LEAF), jnp.float32)
            a_ref[s] = a_ref[s] - mm(col, r_ref[s])
            a_ref[s, at, :] = r_ref[s]
        return carry

    lax.fori_loop(0, n // LEAF, step, 0)
    w_ref[:n, :n] = a_ref[0]
    w_ref[n:, n:] = a_ref[1]
    w_ref[n:, :n] = -mm(a_ref[1], mm(w_ref[n:, :n], a_ref[0]))


def response_kernel(f0, f1, f2, f3, p0, p1, p2, p3, pn_ref, w_ref, v_ref, *, width):
    g = None
    sq = None
    for f, p in ((f0, p0), (f1, p1), (f2, p2), (f3, p3)):
        x = f[...]
        part = mm_nt(x, p[...])
        g = part if g is None else g + part
        xf = x.astype(jnp.float32)
        xs = xf * xf
        sq = xs if sq is None else sq + xs
    n = w_ref.shape[0] // 2
    slab = jnp.exp(-(2.0 / width) * (jnp.sum(sq, axis=1, keepdims=True) + pn_ref[0:1, :] - 2.0 * g))
    v_ref[:, :n] = mm(slab, w_ref[:, :n])
    v_ref[:, n:] = mm(slab[:, n:], w_ref[n:, n:])


def tail_kernel(idx_ref, t_ref, v_ref, w_ref, tp_ref, c_ref, r_ref, parts):
    n, w = tp_ref.shape
    rows = t_ref.shape[0]

    @pl.when(pl.program_id(0) == 0)
    def _():
        delta = mm(w_ref[...], tp_ref[...])
        for i, part in enumerate(split3(delta)):
            parts[:, i * w : (i + 1) * w] = part

    row = lax.broadcasted_iota(jnp.int32, (rows, n), 0) + pl.program_id(0) * rows
    sel = (idx_ref[0:1, :] == row).astype(jnp.bfloat16)
    got = jnp.dot(sel, parts[...], preferred_element_type=jnp.float32)
    coefs = (got[:, :w] + got[:, w : 2 * w]) + got[:, 2 * w :]
    c_ref[...] = coefs
    r_ref[...] = t_ref[...] - mm(v_ref[...], tp_ref[...]) - RIDGE * coefs


def full(shape):
    return pl.BlockSpec(shape, lambda i: (0,) * len(shape))


def tile(rows, width):
    return pl.BlockSpec((rows, width), lambda i: (i, 0))


def pick_points(idx_col, f):
    m, n, w = idx_col.shape[0], *f.shape
    bm = 256
    return pl.pallas_call(
        pick_points_kernel,
        grid=(m // bm,),
        in_specs=[tile(bm, 1), full((n, w))],
        out_specs=tile(bm, w),
        out_shape=jax.ShapeDtypeStruct((m, w), jnp.bfloat16),
        name="pick_points",
    )(idx_col, f)


def pick_targets(idx_col, t):
    m, n, w = idx_col.shape[0], *t.shape
    bm = 256
    return pl.pallas_call(
        pick_targets_kernel,
        grid=(m // bm,),
        in_specs=[tile(bm, 1), full((n, w))],
        out_specs=tile(bm, w),
        out_shape=jax.ShapeDtypeStruct((m, w), jnp.float32),
        scratch_shapes=[pltpu.VMEM((n, 3 * w), jnp.bfloat16)],
        name="pick_targets",
        cost_estimate=pl.CostEstimate(flops=6 * m * n * w, transcendentals=0, bytes_accessed=8 * n * w),
    )(idx_col, t)


def factor(points, width):
    m = points[0].shape[0]
    n = m // 2
    return pl.pallas_call(
        functools.partial(factor_kernel, width=width),
        out_shape=(jax.ShapeDtypeStruct((m, m), jnp.float32), jax.ShapeDtypeStruct((8, m), jnp.float32)),
        scratch_shapes=[pltpu.VMEM((2, n, n), jnp.float32), pltpu.VMEM((2, LEAF, n), jnp.float32)],
        name="factor",
        cost_estimate=pl.CostEstimate(flops=40 * 10**9, transcendentals=0, bytes_accessed=8 * m * m),
    )(*points)


def response(own, points, pn, w, width):
    n = own[0].shape[0]
    m = w.shape[0]
    bm = 256
    return pl.pallas_call(
        functools.partial(response_kernel, width=width),
        grid=(n // bm,),
        in_specs=[tile(bm, x.shape[1]) for x in own]
        + [full(x.shape) for x in points]
        + [full(pn.shape), full(w.shape)],
        out_specs=tile(bm, m),
        out_shape=jax.ShapeDtypeStruct((n, m), jnp.float32),
        name="response",
        cost_estimate=pl.CostEstimate(flops=12 * n * m * m, transcendentals=0, bytes_accessed=8 * m * m),
    )(*own, *points, pn, w)


def tail(idx_row, t, v, w, tp):
    n, width = t.shape
    m = w.shape[0]
    bm = 256
    return pl.pallas_call(
        tail_kernel,
        grid=(n // bm,),
        in_specs=[full(idx_row.shape), tile(bm, width), tile(bm, m), full(w.shape), full(tp.shape)],
        out_specs=(tile(bm, width), tile(bm, width)),
        out_shape=(jax.ShapeDtypeStruct(t.shape, jnp.float32),) * 2,
        scratch_shapes=[pltpu.VMEM((m, 3 * width), jnp.bfloat16)],
        name="tail",
    )(idx_row, t, v, w, tp)


def exchange(parts):
    return lax.all_to_all(parts, ROWS, split_axis=0, concat_axis=0, tiled=True)


def scattered_sum(x, count):
    parts = exchange(x.reshape(count, x.shape[0] // count, x.shape[1]))
    return parts.sum(axis=0)


def gathered(x, count):
    parts = exchange(jnp.broadcast_to(x, (count, *x.shape)))
    return parts.reshape(-1, x.shape[1])


def over_cols(x):
    other = lax.ppermute(x, "xlo", SWAP)
    return (x, other, lax.ppermute(x, "core", SWAP), lax.ppermute(other, "core", SWAP))


def shards(features, targets, block_index):
    rows_here = features.shape[0]
    count = lax.axis_size(ROWS)
    width = features.shape[1] * lax.axis_size(COLS)
    start = lax.axis_index(ROWS) * rows_here
    idx = block_index.reshape(-1) - start
    idx_col = idx[:, None]
    idx_row = jnp.broadcast_to(idx[None, :], (8, idx.shape[0]))
    own = over_cols(features)
    p = gathered(scattered_sum(pick_points(idx_col, features), count), count)
    t = pick_targets(idx_col, targets)
    t, p = lax.optimization_barrier((t, p))
    points = over_cols(p)
    tp = gathered(scattered_sum(t, count), count)
    w, pn = factor(points, width)
    v = response(own, points, pn, w, width)
    return tail(idx_row, targets, v, w, tp)


def solution(mesh):
    split = Mesh(mesh.devices.reshape(2, 8, 4, 2, 2), ROWS + COLS)
    return jax.shard_map(
        shards,
        mesh=split,
        in_specs=(P(ROWS, COLS), P(ROWS, COLS), P()),
        out_specs=(P(ROWS, COLS), P(ROWS, COLS)),
        check_vma=False,
    )
```

```python
import functools

import jax
import jax.numpy as jnp
from jax import lax
from jax.experimental import pallas as pl
from jax.experimental.pallas import tpu as pltpu
from jax.sharding import Mesh
from jax.sharding import PartitionSpec as P

ROWS = ("r0", "r1", "r2")
COLS = ("xlo", "core")
RIDGE = 1.0
LEAF = 128
HI = lax.Precision.HIGHEST
SWAP = [(0, 1), (1, 0)]
SLOTS = 32
CAP = 96


def mm(a, b):
    return lax.dot_general(a, b, (((1,), (0,)), ((), ())), precision=HI, preferred_element_type=jnp.float32)


def mm_nt(a, b):
    return lax.dot_general(a, b, (((1,), (1,)), ((), ())), preferred_element_type=jnp.float32)


def inv2(a, b, d):
    i = 1.0 / (a * d - b * b)
    return d * i, -b * i, a * i


def leaf_inverse(m):
    n = m.shape[-1]
    lane = lax.broadcasted_iota(jnp.int32, (1, 1, n), 2)
    sub = lax.broadcasted_iota(jnp.int32, (1, n, 1), 1)
    for j in range(0, n, 4):
        c = [jnp.broadcast_to(m[:, :, j + q : j + q + 1], m.shape) for q in range(4)]
        e = lambda p, q: c[q][:, j + p : j + p + 1, :]
        r = []
        for q in range(4):
            row = m[:, j + q : j + q + 1, :]
            for w in range(4):
                row = jnp.where(lane == j + w, 1.0 if w == q else 0.0, row)
            r.append(row)
        x11, x12, x22 = inv2(e(0, 0), e(0, 1), e(1, 1))
        b = [[e(0, 2), e(0, 3)], [e(1, 2), e(1, 3)]]
        y = [
            [x11 * b[0][q] + x12 * b[1][q] for q in range(2)],
            [x12 * b[0][q] + x22 * b[1][q] for q in range(2)],
        ]
        s = lambda p, q, base: base - (b[0][p] * y[0][q] + b[1][p] * y[1][q])
        z11, z12, z22 = inv2(s(0, 0, e(2, 2)), s(0, 1, e(2, 3)), s(1, 1, e(3, 3)))
        w0 = x11 * r[0] + x12 * r[1]
        w1 = x12 * r[0] + x22 * r[1]
        t0 = r[2] - (b[0][0] * w0 + b[1][0] * w1)
        t1 = r[3] - (b[0][1] * w0 + b[1][1] * w1)
        s2 = z11 * t0 + z12 * t1
        s3 = z12 * t0 + z22 * t1
        s0 = w0 - (y[0][0] * s2 + y[0][1] * s3)
        s1 = w1 - (y[1][0] * s2 + y[1][1] * s3)
        new = jnp.where((lane >= j) & (lane < j + 4), 0.0, m)
        new = new - ((c[0] * s0 + c[1] * s1) + (c[2] * s2 + c[3] * s3))
        for q, sq in enumerate((s0, s1, s2, s3)):
            new = jnp.where(sub == j + q, sq, new)
        m = new
    return m


def leaf_inverse_small(m):
    n = m.shape[-1]
    lane = lax.broadcasted_iota(jnp.int32, (1, 1, n), 2)
    sub = lax.broadcasted_iota(jnp.int32, (1, n, 1), 1)

    def step(j, m):
        c = jnp.sum(jnp.where(lane == j, m, 0.0), axis=2, keepdims=True)
        r = jnp.sum(jnp.where(sub == j, m, 0.0), axis=1, keepdims=True)
        ip = 1.0 / jnp.sum(jnp.where(lane == j, r, 0.0), axis=2, keepdims=True)
        r = jnp.where(lane == j, ip, r * ip)
        return jnp.where(sub == j, r, jnp.where(lane == j, 0.0, m) - c * r)

    return lax.fori_loop(0, n, step, m)


def pick_points_kernel(idx_ref, f_ref, o_ref):
    n = f_ref.shape[0]
    sel = (idx_ref[...] == lax.broadcasted_iota(jnp.int32, (idx_ref.shape[0], n), 1)).astype(jnp.bfloat16)
    o_ref[...] = jnp.dot(sel, f_ref[...], preferred_element_type=jnp.float32).astype(jnp.bfloat16)


def split3(x):
    hi = x.astype(jnp.bfloat16)
    rest = x - hi.astype(jnp.float32)
    mid = rest.astype(jnp.bfloat16)
    low = (rest - mid.astype(jnp.float32)).astype(jnp.bfloat16)
    return hi, mid, low


def pick_targets_kernel(idx_ref, t_ref, o_ref, parts):
    n, w = t_ref.shape

    @pl.when(pl.program_id(0) == 0)
    def _():
        for i, part in enumerate(split3(t_ref[...])):
            parts[:, i * w : (i + 1) * w] = part

    sel = (idx_ref[...] == lax.broadcasted_iota(jnp.int32, (idx_ref.shape[0], n), 1)).astype(jnp.bfloat16)
    got = jnp.dot(sel, parts[...], preferred_element_type=jnp.float32)
    o_ref[...] = (got[:, :w] + got[:, w : 2 * w]) + got[:, 2 * w :]


def invert_blocks(a_ref, r_ref, leaf):
    n = a_ref.shape[1]

    def step(k, carry):
        at = pl.ds(pl.multiple_of(k * LEAF, LEAF), LEAF)
        dinv = leaf(a_ref[:, at, at])
        for s in range(2):
            r_ref[s] = mm(dinv[s], a_ref[s, at, :])
            r_ref[s, :, at] = dinv[s]
            col = a_ref[s, :, at]
            a_ref[s, :, at] = jnp.zeros((n, LEAF), jnp.float32)
            a_ref[s] = a_ref[s] - mm(col, r_ref[s])
            a_ref[s, at, :] = r_ref[s]
        return carry

    lax.fori_loop(0, n // LEAF, step, 0)


def factor_kernel(p0, p1, p2, p3, k_ref, pn_ref, a_ref, r_ref, *, width, leaf):
    points = (p0, p1, p2, p3)
    n = p0.shape[0] // 2
    gram = lambda a, b: sum(mm_nt(p[a * n : (a + 1) * n, :], p[b * n : (b + 1) * n, :]) for p in points)
    eye = lax.broadcasted_iota(jnp.int32, (n, n), 0) == lax.broadcasted_iota(jnp.int32, (n, n), 1)
    scale = -(2.0 / width)
    rows, cols = [], []
    for s in range(2):
        g = gram(s, s)
        diag = jnp.where(eye, g, 0.0)
        rows.append(jnp.sum(diag, axis=0, keepdims=True))
        cols.append(jnp.sum(diag, axis=1, keepdims=True))
        k = jnp.exp(scale * (cols[s] + rows[s] - 2.0 * g))
        a_ref[s] = k + jnp.where(eye, RIDGE, 0.0)
        pn_ref[:, s * n : (s + 1) * n] = jnp.broadcast_to(rows[s], (8, n))
    k_ref[...] = jnp.exp(scale * (cols[1] + rows[0] - 2.0 * gram(1, 0)))
    invert_blocks(a_ref, r_ref, leaf)


def split2(x):
    hi = x.astype(jnp.bfloat16)
    return hi, (x - hi.astype(jnp.float32)).astype(jnp.bfloat16)


def slab_kernel(f0, f1, f2, f3, p0, p1, p2, p3, pn_ref, s_ref, *, width):
    g = None
    sq = None
    for f, p in ((f0, p0), (f1, p1), (f2, p2), (f3, p3)):
        x = f[...]
        part = mm_nt(x, p[...])
        g = part if g is None else g + part
        xf = x.astype(jnp.float32)
        xs = xf * xf
        sq = xs if sq is None else sq + xs
    m = p0.shape[0]
    slab = jnp.exp(-(2.0 / width) * (jnp.sum(sq, axis=1, keepdims=True) + pn_ref[0:1, :] - 2.0 * g))
    s_ref[:, :m], s_ref[:, m:] = split2(slab)


def solve_into(tp, x_ref, k_ref, delta, parts):
    n = x_ref.shape[1]
    w = delta.shape[1]
    first = mm(x_ref[0], tp[0:n, :])
    second = mm(x_ref[1], tp[n : 2 * n, :] - mm(k_ref[...], first))
    delta[0:n, :] = first
    delta[n : 2 * n, :] = second
    parts[0:n, :w], parts[0:n, w:] = split2(first)
    parts[n : 2 * n, :w], parts[n : 2 * n, w:] = split2(second)


def fitted(s_ref, parts):
    m, w = parts.shape[0], parts.shape[1] // 2
    both = jnp.dot(s_ref[:, :m], parts[...], preferred_element_type=jnp.float32)
    low = jnp.dot(s_ref[:, m:], parts[:, :w], preferred_element_type=jnp.float32)
    return both[:, :w] + (both[:, w:] + low)


def lay_out(counts, b_ref, dense):
    groups = counts.shape[0] // 2
    lanes = dense.shape[1]
    row = lax.broadcasted_iota(jnp.int32, (CAP + 8, lanes), 0)
    for s in range(2):
        at = jnp.int32(s * ((dense.shape[0] - CAP - 8) // 2))
        for g in range(groups):
            src = (2 * g + s) * CAP
            shift = at & 7
            window = pl.ds(pl.multiple_of(at - shift, 8), CAP + 8)
            x = jnp.concatenate([b_ref[src : src + CAP, :], b_ref[src : src + 8, :]], axis=0)
            dense[window, :] = jnp.where(row >= shift, pltpu.roll(x, shift, 0), dense[window, :])
            at = at + counts[2 * g + s]


def dense_points_kernel(counts, b_ref, o_ref, wide, dense):
    wide[...] = b_ref[...].astype(jnp.float32)

    lay_out(counts, wide, dense)
    o_ref[...] = dense[0 : o_ref.shape[0], :].astype(jnp.bfloat16)


def tail_kernel(counts, own_row, own_pos, t_ref, s_ref, x_ref, k_ref, b_ref, c_ref, r_ref, tp, delta, parts):
    rows = t_ref.shape[0]
    base = pl.program_id(0) * rows

    @pl.when(pl.program_id(0) == 0)
    def _():
        lay_out(counts, b_ref, tp)
        solve_into(tp, x_ref, k_ref, delta, parts)

    c_ref[...] = jnp.zeros(c_ref.shape, jnp.float32)
    r_ref[...] = t_ref[...] - fitted(s_ref, parts)
    for q in range(SLOTS):
        row = own_row[q] - base

        @pl.when((row >= 0) & (row < rows))
        def _():
            got = delta[pl.ds(own_pos[q], 1), :]
            c_ref[pl.ds(row, 1), :] = got
            r_ref[pl.ds(row, 1), :] = r_ref[pl.ds(row, 1), :] - RIDGE * got


def slow_tail_kernel(idx_ref, t_ref, s_ref, x_ref, k_ref, tp_ref, c_ref, r_ref, delta, parts, exact):
    n, w = tp_ref.shape
    rows = t_ref.shape[0]

    @pl.when(pl.program_id(0) == 0)
    def _():
        solve_into(tp_ref, x_ref, k_ref, delta, parts)
        for i, part in enumerate(split3(delta[...])):
            exact[:, i * w : (i + 1) * w] = part

    row = lax.broadcasted_iota(jnp.int32, (rows, n), 0) + pl.program_id(0) * rows
    sel = (idx_ref[0:1, :] == row).astype(jnp.bfloat16)
    got = jnp.dot(sel, exact[...], preferred_element_type=jnp.float32)
    coefs = (got[:, :w] + got[:, w : 2 * w]) + got[:, 2 * w :]
    c_ref[...] = coefs
    r_ref[...] = t_ref[...] - fitted(s_ref, parts) - RIDGE * coefs


def prefix(mask, tri):
    n, total = mask.shape[0], jnp.zeros((mask.shape[0], 1), jnp.float32)
    out = []
    for b in range(mask.shape[1] // 128):
        part = mask[:, b * 128 : (b + 1) * 128]
        out.append(jnp.dot(part.astype(jnp.bfloat16), tri, preferred_element_type=jnp.float32) + total)
        total = total + jnp.sum(part, axis=1, keepdims=True)
    return jnp.concatenate(out, axis=1), total


def plan_kernel(me, b_ref, f_ref, own_ref, list_ref, count_ref, p_ref, *, shift, far, mid, near):
    xh, z, y = me[0], me[1], me[2]
    lanes = b_ref.shape[1]
    idx = jnp.concatenate([b_ref[0:1, :], b_ref[1:2, :]], axis=1)
    m = idx.shape[1]
    one = lambda c: jnp.where(c, 1.0, 0.0)
    owner = lax.shift_right_logical(idx, shift)
    row = (idx & ((1 << shift) - 1)).astype(jnp.float32)
    hi = owner // (mid * near)
    oz = (owner // near) % mid
    oy = owner % near
    group = hi * near + oy
    my_group = xh * near + y
    step = (lax.broadcasted_iota(jnp.int32, (1, m), 1) >= lanes).astype(jnp.int32)
    tri = one(
        lax.broadcasted_iota(jnp.int32, (128, 128), 0) < lax.broadcasted_iota(jnp.int32, (128, 128), 1)
    ).astype(jnp.bfloat16)
    mine = group == my_group
    masks = one((oz == lax.broadcasted_iota(jnp.int32, (mid, m), 0)) & mine)
    rank_all, _ = prefix(masks, tri)
    rank = jnp.sum(rank_all * masks, axis=0, keepdims=True)
    cls = one((step == lax.broadcasted_iota(jnp.int32, (8, m), 0)) & mine)
    crank_all, _ = prefix(cls, tri)
    crank = jnp.sum(crank_all * cls, axis=0, keepdims=True)
    own = mine & (oz == z)
    slot = lax.broadcasted_iota(jnp.int32, (SLOTS, m), 0).astype(jnp.float32)
    hit = own & (slot == rank)
    before = one(group < my_group)
    early = (step == 0).astype(jnp.float32)
    off0 = jnp.sum(before * early, axis=1, keepdims=True)
    off1 = jnp.sum(before * (1.0 - early), axis=1, keepdims=True)
    pos = jnp.where(step == 0, off0, off1 + float(lanes)) + crank
    take = lambda hits, v: jnp.sum(jnp.where(hits, v + 1.0, 0.0), axis=1, keepdims=True) - 1.0
    own_row = take(hit, row)
    column = lax.broadcasted_iota(jnp.int32, (SLOTS, 128), 1)
    both = jnp.where(column == 0, own_row, take(hit, pos))
    own_ref[...] = both.astype(jnp.int32)
    v = oz.astype(jnp.float32) * float(SLOTS) + rank
    for s in range(2):
        half = slice(s * lanes, (s + 1) * lanes)
        u = lax.broadcasted_iota(jnp.int32, (CAP, lanes), 0).astype(jnp.float32)
        got = take(mine[:, half] & (u == crank[:, half]), v[:, half])
        list_ref[s * CAP : (s + 1) * CAP, :] = jnp.broadcast_to(got, (CAP, 128)).astype(jnp.int32)
    code = 2 * group + step
    classes = 2 * far * near
    count = jnp.sum(one(code == lax.broadcasted_iota(jnp.int32, (classes, m), 0)), axis=1, keepdims=True)
    owners = far * mid * near
    used = jnp.sum(one(owner == lax.broadcasted_iota(jnp.int32, (owners, m), 0)), axis=1, keepdims=True)
    over = one(jnp.max(used, axis=0, keepdims=True) > float(SLOTS)) + one(
        jnp.max(count, axis=0, keepdims=True) > float(CAP)
    )
    count_ref[0:classes, :] = jnp.broadcast_to(count, (classes, 128)).astype(jnp.int32)
    count_ref[classes:, :] = jnp.broadcast_to(over, (8, 128)).astype(jnp.int32)
    n = f_ref.shape[0]
    at = lax.broadcasted_iota(jnp.int32, (SLOTS, n), 1).astype(jnp.float32)
    sel = one(own_row == at).astype(jnp.bfloat16)
    p_ref[...] = jnp.dot(sel, f_ref[...], preferred_element_type=jnp.float32).astype(jnp.bfloat16)


def own_targets_kernel(own_row, t_ref, o_ref):
    for q in range(SLOTS):
        row = own_row[q]
        got = t_ref[pl.ds(jnp.maximum(row, 0), 1), :]
        o_ref[q : q + 1, :] = jnp.where(row >= 0, got, 0.0)


def pack_kernel(list_ref, b_ref, o_ref):
    m, n = list_ref.shape[0], b_ref.shape[0]
    sel = jnp.where(list_ref[:, 0:1] == lax.broadcasted_iota(jnp.int32, (m, n), 1), 1.0, 0.0).astype(jnp.bfloat16)
    b = b_ref[...]
    if b.dtype == jnp.bfloat16:
        o_ref[...] = jnp.dot(sel, b, preferred_element_type=jnp.float32).astype(jnp.bfloat16)
    else:
        hi, mid, low = (jnp.dot(sel, part, preferred_element_type=jnp.float32) for part in split3(b))
        o_ref[...] = (hi + mid) + low


def full(shape):
    return pl.BlockSpec(shape, lambda i: (0,) * len(shape))


def tile(rows, width):
    return pl.BlockSpec((rows, width), lambda i: (i, 0))


def pick_points(idx_col, f):
    m, n, w = idx_col.shape[0], *f.shape
    bm = 256
    return pl.pallas_call(
        pick_points_kernel,
        grid=(m // bm,),
        in_specs=[tile(bm, 1), full((n, w))],
        out_specs=tile(bm, w),
        out_shape=jax.ShapeDtypeStruct((m, w), jnp.bfloat16),
        name="pick_points",
    )(idx_col, f)


def pick_targets(idx_col, t):
    m, n, w = idx_col.shape[0], *t.shape
    bm = 256
    return pl.pallas_call(
        pick_targets_kernel,
        grid=(m // bm,),
        in_specs=[tile(bm, 1), full((n, w))],
        out_specs=tile(bm, w),
        out_shape=jax.ShapeDtypeStruct((m, w), jnp.float32),
        scratch_shapes=[pltpu.VMEM((n, 3 * w), jnp.bfloat16)],
        name="pick_targets",
        cost_estimate=pl.CostEstimate(flops=6 * m * n * w, transcendentals=0, bytes_accessed=8 * n * w),
    )(idx_col, t)


def factor(points, width, leaf):
    m = points[0].shape[0]
    n = m // 2
    return pl.pallas_call(
        functools.partial(factor_kernel, width=width, leaf=leaf),
        out_shape=(
            jax.ShapeDtypeStruct((n, n), jnp.float32),
            jax.ShapeDtypeStruct((8, m), jnp.float32),
            jax.ShapeDtypeStruct((2, n, n), jnp.float32),
        ),
        in_specs=[pl.BlockSpec(memory_space=pltpu.VMEM)] * 4,
        out_specs=(pl.BlockSpec(memory_space=pltpu.VMEM),) * 3,
        scratch_shapes=[pltpu.VMEM((2, LEAF, n), jnp.float32)],
        name="factor",
        cost_estimate=pl.CostEstimate(flops=40 * 10**9, transcendentals=0, bytes_accessed=8 * m * m),
    )(*points)


def slab_of(own, points, pn, width):
    n = own[0].shape[0]
    m = points[0].shape[0]
    bm = 256
    return pl.pallas_call(
        functools.partial(slab_kernel, width=width),
        grid=(n // bm,),
        in_specs=[tile(bm, x.shape[1]) for x in own] + [full(x.shape) for x in points] + [full(pn.shape)],
        out_specs=tile(bm, 2 * m),
        out_shape=jax.ShapeDtypeStruct((n, 2 * m), jnp.bfloat16),
        name="slab",
        cost_estimate=pl.CostEstimate(flops=2 * n * m * width, transcendentals=0, bytes_accessed=8 * n * m),
    )(*own, *points, pn)


SMEM = pl.BlockSpec(memory_space=pltpu.SMEM)


def tail(counts, own_row, own_pos, t, slab, x, k, buffer):
    n, width = t.shape
    m = 2 * k.shape[0]
    bm = 256
    return pl.pallas_call(
        tail_kernel,
        grid=(n // bm,),
        in_specs=[SMEM, SMEM, SMEM, tile(bm, width), tile(bm, 2 * m), full(x.shape), full(k.shape), full(buffer.shape)],
        out_specs=(tile(bm, width), tile(bm, width)),
        out_shape=(jax.ShapeDtypeStruct(t.shape, jnp.float32),) * 2,
        scratch_shapes=[
            pltpu.VMEM((m + CAP + 8, width), jnp.float32),
            pltpu.VMEM((m, width), jnp.float32),
            pltpu.VMEM((m, 2 * width), jnp.bfloat16),
        ],
        name="tail",
    )(counts, own_row, own_pos, t, slab, x, k, buffer)


def slow_tail(idx_row, t, slab, x, k, tp):
    n, width = t.shape
    m = tp.shape[0]
    bm = 256
    return pl.pallas_call(
        slow_tail_kernel,
        grid=(n // bm,),
        in_specs=[full(idx_row.shape), tile(bm, width), tile(bm, 2 * m), full(x.shape), full(k.shape), full(tp.shape)],
        out_specs=(tile(bm, width), tile(bm, width)),
        out_shape=(jax.ShapeDtypeStruct(t.shape, jnp.float32),) * 2,
        scratch_shapes=[
            pltpu.VMEM((m, width), jnp.float32),
            pltpu.VMEM((m, 2 * width), jnp.bfloat16),
            pltpu.VMEM((m, 3 * width), jnp.bfloat16),
        ],
        name="slow_tail",
    )(idx_row, t, slab, x, k, tp)


def plan(me, block_index, f, sizes):
    far, mid, near = sizes
    n, w = f.shape
    vmem = pl.BlockSpec(memory_space=pltpu.VMEM)
    i32 = jnp.int32
    return pl.pallas_call(
        functools.partial(plan_kernel, shift=n.bit_length() - 1, far=far, mid=mid, near=near),
        in_specs=[SMEM, vmem, vmem],
        out_specs=(vmem,) * 4,
        out_shape=(
            jax.ShapeDtypeStruct((SLOTS, 128), i32),
            jax.ShapeDtypeStruct((2 * CAP, 128), i32),
            jax.ShapeDtypeStruct((2 * far * near + 8, 128), i32),
            jax.ShapeDtypeStruct((SLOTS, w), f.dtype),
        ),
        name="plan",
    )(me, block_index, f)


def own_targets(own_row, t):
    return pl.pallas_call(
        own_targets_kernel,
        in_specs=[SMEM, pl.BlockSpec(memory_space=pltpu.VMEM)],
        out_specs=pl.BlockSpec(memory_space=pltpu.VMEM),
        out_shape=jax.ShapeDtypeStruct((SLOTS, t.shape[1]), t.dtype),
        name="own_targets",
    )(own_row, t)


def pack(where, buffer):
    vmem = pl.BlockSpec(memory_space=pltpu.VMEM)
    return pl.pallas_call(
        pack_kernel,
        in_specs=[vmem, vmem],
        out_specs=vmem,
        out_shape=jax.ShapeDtypeStruct((where.shape[0], buffer.shape[1]), buffer.dtype),
        name="pack",
    )(where, buffer)


def dense_points(counts, buffer, m):
    w = buffer.shape[1]
    vmem = pl.BlockSpec(memory_space=pltpu.VMEM)
    return pl.pallas_call(
        dense_points_kernel,
        in_specs=[SMEM, vmem],
        out_specs=vmem,
        out_shape=jax.ShapeDtypeStruct((m, w), buffer.dtype),
        scratch_shapes=[pltpu.VMEM(buffer.shape, jnp.float32), pltpu.VMEM((m + CAP + 8, w), jnp.float32)],
        name="dense_points",
    )(counts, buffer)


def spread(x, axes):
    parts = jnp.broadcast_to(x, (lax.axis_size(axes), *x.shape))
    parts = lax.all_to_all(parts, axes, split_axis=0, concat_axis=0, tiled=True)
    return parts.reshape(-1, x.shape[1])


def exchange(parts):
    return lax.all_to_all(parts, ROWS, split_axis=0, concat_axis=0, tiled=True)


def scattered_sum(x, count):
    parts = exchange(x.reshape(count, x.shape[0] // count, x.shape[1]))
    return parts.sum(axis=0)


def gathered(x, count):
    parts = exchange(jnp.broadcast_to(x, (count, *x.shape)))
    return parts.reshape(-1, x.shape[1])


def over_cols(x):
    other = lax.ppermute(x, "xlo", SWAP)
    return (x, other, lax.ppermute(x, "core", SWAP), lax.ppermute(other, "core", SWAP))


def slow(features, targets, block_index):
    rows_here = features.shape[0]
    count = lax.axis_size(ROWS)
    width = features.shape[1] * lax.axis_size(COLS)
    idx = block_index.reshape(-1) - lax.axis_index(ROWS) * rows_here
    idx_col = idx[:, None]
    idx_row = jnp.broadcast_to(idx[None, :], (8, idx.shape[0]))
    own = over_cols(features)
    points = over_cols(gathered(scattered_sum(pick_points(idx_col, features), count), count))
    tp = gathered(scattered_sum(pick_targets(idx_col, targets), count), count)
    k, pn, x = factor(points, width, leaf_inverse_small)
    return tuple(slow_tail(idx_row, targets, slab_of(own, points, pn, width), x, k, tp))


def shards(features, targets, block_index):
    width = features.shape[1] * lax.axis_size(COLS)
    sizes = tuple(lax.axis_size(a) for a in ROWS)
    me = jnp.stack([lax.axis_index(a) for a in ROWS]).astype(jnp.int32)
    across = (ROWS[0], ROWS[2])
    own_list, where, counts, p = plan(me, block_index, features, sizes)
    own_row, own_pos = own_list[:, 0], own_list[:, 1]
    classes = counts.shape[0] - 8
    overflow = counts[classes, 0] > 0
    counts = counts[:classes, 0]
    own = over_cols(features)
    p = pack(where, spread(p, ROWS[1]))
    p = dense_points(counts, spread(p, across), block_index.size)
    t, p = lax.optimization_barrier((own_targets(own_row, targets), p))
    points = over_cols(p)
    t = spread(pack(where, spread(t, ROWS[1])), across)
    k, pn, x = factor(points, width, leaf_inverse)
    slab = slab_of(own, points, pn, width)
    return lax.cond(
        overflow,
        lambda: slow(features, targets, block_index),
        lambda: tuple(tail(counts, own_row, own_pos, targets, slab, x, k, t)),
    )


def solution(mesh):
    split = Mesh(mesh.devices.reshape(2, 8, 4, 2, 2), ROWS + COLS)
    return jax.shard_map(
        shards,
        mesh=split,
        in_specs=(P(ROWS, COLS), P(ROWS, COLS), P()),
        out_specs=(P(ROWS, COLS), P(ROWS, COLS)),
        check_vma=False,
    )
```

```python
import functools

import jax
import jax.numpy as jnp
from jax import lax
from jax.experimental import pallas as pl
from jax.experimental.pallas import tpu as pltpu
from jax.sharding import Mesh
from jax.sharding import PartitionSpec as P

ROWS = ("r0", "r1", "r2")
COLS = ("xlo", "core")
RIDGE = 1.0
LEAF = 128
SWAP = [(0, 1), (1, 0)]
SLOTS = 32
CAP = 96


def dot(a, b):
    return jnp.dot(a, b, preferred_element_type=jnp.float32)


def mm6(a, b):
    a0, a1, a2 = split3(a)
    b0, b1, b2 = split3(b)
    return dot(
        jnp.concatenate([a2, a1, a0, a1, a0, a0], axis=1),
        jnp.concatenate([b0, b1, b2, b0, b1, b0], axis=0),
    )


def mm_nt(a, b):
    return lax.dot_general(a, b, (((1,), (1,)), ((), ())), preferred_element_type=jnp.float32)


def inv2(a, b, d):
    i = 1.0 / (a * d - b * b)
    return d * i, -b * i, a * i


def leaf_inverse(m):
    n = m.shape[-1]
    lane = lax.broadcasted_iota(jnp.int32, (1, 1, n), 2)
    sub = lax.broadcasted_iota(jnp.int32, (1, n, 1), 1)
    for j in range(0, n, 4):
        c = [jnp.broadcast_to(m[:, :, j + q : j + q + 1], m.shape) for q in range(4)]
        e = lambda p, q: c[q][:, j + p : j + p + 1, :]
        r = []
        for q in range(4):
            row = m[:, j + q : j + q + 1, :]
            for w in range(4):
                row = jnp.where(lane == j + w, 1.0 if w == q else 0.0, row)
            r.append(row)
        x11, x12, x22 = inv2(e(0, 0), e(0, 1), e(1, 1))
        b = [[e(0, 2), e(0, 3)], [e(1, 2), e(1, 3)]]
        y = [
            [x11 * b[0][q] + x12 * b[1][q] for q in range(2)],
            [x12 * b[0][q] + x22 * b[1][q] for q in range(2)],
        ]
        s = lambda p, q, base: base - (b[0][p] * y[0][q] + b[1][p] * y[1][q])
        z11, z12, z22 = inv2(s(0, 0, e(2, 2)), s(0, 1, e(2, 3)), s(1, 1, e(3, 3)))
        w0 = x11 * r[0] + x12 * r[1]
        w1 = x12 * r[0] + x22 * r[1]
        t0 = r[2] - (b[0][0] * w0 + b[1][0] * w1)
        t1 = r[3] - (b[0][1] * w0 + b[1][1] * w1)
        s2 = z11 * t0 + z12 * t1
        s3 = z12 * t0 + z22 * t1
        s0 = w0 - (y[0][0] * s2 + y[0][1] * s3)
        s1 = w1 - (y[1][0] * s2 + y[1][1] * s3)
        new = jnp.where((lane >= j) & (lane < j + 4), 0.0, m)
        new = new - ((c[0] * s0 + c[1] * s1) + (c[2] * s2 + c[3] * s3))
        for q, sq in enumerate((s0, s1, s2, s3)):
            new = jnp.where(sub == j + q, sq, new)
        m = new
    return m


def invert_by_pivots(a_ref):
    n = a_ref.shape[-1]
    lane = lax.broadcasted_iota(jnp.int32, (1, 1, n), 2)
    strip = 64
    high = lax.broadcasted_iota(jnp.int32, (1, strip, 1), 1)

    def step(j, carry):
        r = a_ref[:, pl.ds(j, 1), :]
        ip = 1.0 / jnp.sum(jnp.where(lane == j, r, 0.0), axis=2, keepdims=True)
        r = jnp.where(lane == j, ip, r * ip)

        def rows(i, carry):
            here = pl.ds(pl.multiple_of(i * strip, strip), strip)
            x = a_ref[:, here, :]
            c = jnp.sum(jnp.where(lane == j, x, 0.0), axis=2, keepdims=True)
            x = jnp.where(lane == j, 0.0, x) - c * r
            a_ref[:, here, :] = jnp.where(high + i * strip == j, r, x)
            return carry

        return lax.fori_loop(0, n // strip, rows, carry)

    lax.fori_loop(0, n, step, 0)


def pick_points_kernel(idx_ref, f_ref, o_ref):
    n = f_ref.shape[0]
    sel = (idx_ref[...] == lax.broadcasted_iota(jnp.int32, (idx_ref.shape[0], n), 1)).astype(jnp.bfloat16)
    o_ref[...] = jnp.dot(sel, f_ref[...], preferred_element_type=jnp.float32).astype(jnp.bfloat16)


def split3(x):
    hi = x.astype(jnp.bfloat16)
    rest = x - hi.astype(jnp.float32)
    mid = rest.astype(jnp.bfloat16)
    low = (rest - mid.astype(jnp.float32)).astype(jnp.bfloat16)
    return hi, mid, low


def pick_targets_kernel(idx_ref, t_ref, o_ref, parts):
    n, w = t_ref.shape

    @pl.when(pl.program_id(0) == 0)
    def _():
        for i, part in enumerate(split3(t_ref[...])):
            parts[:, i * w : (i + 1) * w] = part

    sel = (idx_ref[...] == lax.broadcasted_iota(jnp.int32, (idx_ref.shape[0], n), 1)).astype(jnp.bfloat16)
    got = jnp.dot(sel, parts[...], preferred_element_type=jnp.float32)
    o_ref[...] = (got[:, :w] + got[:, w : 2 * w]) + got[:, 2 * w :]


def factor_kernel(p0, p1, p2, p3, f0, f1, f2, f3, k_ref, x_ref, s_ref, a_ref, r_ref, c_ref, d_ref, *, width, blocked):
    points, own = (p0, p1, p2, p3), (f0, f1, f2, f3)
    m = p0.shape[0]
    n = m // 2
    gram = lambda a, b: sum(mm_nt(p[a * n : (a + 1) * n, :], p[b * n : (b + 1) * n, :]) for p in points)
    eye = lax.broadcasted_iota(jnp.int32, (n, n), 0) == lax.broadcasted_iota(jnp.int32, (n, n), 1)
    scale = -(2.0 / width)
    rows, cols = [], []
    for s in range(2):
        g = gram(s, s)
        diag = jnp.where(eye, g, 0.0)
        rows.append(jnp.sum(diag, axis=0, keepdims=True))
        cols.append(jnp.sum(diag, axis=1, keepdims=True))
        k = jnp.exp(scale * (cols[s] + rows[s] - 2.0 * g))
        a_ref[s] = k + jnp.where(eye, RIDGE, 0.0)
    k_ref[:, :n], k_ref[:, n:] = split2(jnp.exp(scale * (cols[1] + rows[0] - 2.0 * gram(1, 0))))
    point_sq = jnp.concatenate(rows, axis=1)
    d_ref[...] = a_ref[:, 0:LEAF, 0:LEAF]
    c_ref[...] = jnp.zeros(c_ref.shape, jnp.float32)
    r_ref[...] = jnp.zeros(r_ref.shape, jnp.float32)
    blocks = n // LEAF
    tile_rows = f0.shape[0] // blocks

    def slab_tile(k):
        here = pl.ds(pl.multiple_of(k * tile_rows, tile_rows), tile_rows)
        g, sq = 0.0, 0.0
        for f, p in zip(own, points):
            x = f[here, :]
            g = g + mm_nt(x, p[...])
            xf = x.astype(jnp.float32)
            sq = sq + xf * xf
        slab = jnp.exp(scale * (jnp.sum(sq, axis=1, keepdims=True) + point_sq - 2.0 * g))
        s_ref[here, :m], s_ref[here, m:] = split2(slab)

    def step(k, carry):
        block = lambda i: pl.ds(pl.multiple_of(i * LEAF, LEAF), LEAF)
        at, ahead, last = block(k), block(jnp.minimum(k + 1, blocks - 1)), block(jnp.maximum(k - 1, 0))
        if not blocked:
            slab_tile(k)
            return carry
        dinv = leaf_inverse(d_ref[...])
        for s in range(2):
            a_ref[s] = a_ref[s] - mm6(c_ref[s], r_ref[s])

        @pl.when(k > 0)
        def _():
            for s in range(2):
                a_ref[s, last, :] = r_ref[s]

        slab_tile(k)
        for s in range(2):
            r_ref[s] = mm6(dinv[s], a_ref[s, at, :])
            r_ref[s, :, at] = dinv[s]
            c_ref[s] = a_ref[s, :, at]
            a_ref[s, :, at] = jnp.zeros((n, LEAF), jnp.float32)
            d_ref[s] = a_ref[s, ahead, ahead] - mm6(c_ref[s, ahead, :], r_ref[s, :, ahead])
        return carry

    lax.fori_loop(0, blocks, step, 0)
    if not blocked:
        invert_by_pivots(a_ref)
        for s in range(2):
            x_ref[s, :, :n], x_ref[s, :, n:] = split2(a_ref[s])
        return
    for s in range(2):
        done = a_ref[s] - mm6(c_ref[s], r_ref[s])
        x_ref[s, :, :n], x_ref[s, :, n:] = split2(done)
        x_ref[s, n - LEAF : n, :n], x_ref[s, n - LEAF : n, n:] = split2(r_ref[s])


def split2(x):
    hi = x.astype(jnp.bfloat16)
    return hi, (x - hi.astype(jnp.float32)).astype(jnp.bfloat16)


def product3(a_pair, b):
    k = a_pair.shape[1] // 2
    hi, low = split2(b)
    both = dot(a_pair[:, :k], jnp.concatenate([hi, low], axis=1))
    return both[:, : b.shape[1]] + (both[:, b.shape[1] :] + dot(a_pair[:, k:], hi))


def solve_into(tp, x_ref, k_ref, delta, parts):
    n = x_ref.shape[1]
    w = delta.shape[1]
    first = product3(x_ref[0], tp[0:n, :])
    second = product3(x_ref[1], tp[n : 2 * n, :] - product3(k_ref[...], first))
    delta[0:n, :] = first
    delta[n : 2 * n, :] = second
    parts[0:n, :w], parts[0:n, w:] = split2(first)
    parts[n : 2 * n, :w], parts[n : 2 * n, w:] = split2(second)


def fitted(s_ref, parts):
    m, w = parts.shape[0], parts.shape[1] // 2
    both = jnp.dot(s_ref[:, :m], parts[...], preferred_element_type=jnp.float32)
    low = jnp.dot(s_ref[:, m:], parts[:, :w], preferred_element_type=jnp.float32)
    return both[:, :w] + (both[:, w:] + low)


def lay_out(counts, b_ref, dense):
    groups = counts.shape[0] // 2
    lanes = dense.shape[1]
    row = lax.broadcasted_iota(jnp.int32, (CAP + 8, lanes), 0)
    for s in range(2):
        at = jnp.int32(s * ((dense.shape[0] - CAP - 8) // 2))
        for g in range(groups):
            src = (2 * g + s) * CAP
            shift = at & 7
            window = pl.ds(pl.multiple_of(at - shift, 8), CAP + 8)
            x = jnp.concatenate([b_ref[src : src + CAP, :], b_ref[src : src + 8, :]], axis=0)
            dense[window, :] = jnp.where(row >= shift, pltpu.roll(x, shift, 0), dense[window, :])
            at = at + counts[2 * g + s]


def dense_points_kernel(counts, b_ref, o_ref, wide, dense):
    wide[...] = b_ref[...].astype(jnp.float32)

    lay_out(counts, wide, dense)
    o_ref[...] = dense[0 : o_ref.shape[0], :].astype(jnp.bfloat16)


def tail_kernel(counts, own_row, own_pos, t_ref, s_ref, x_ref, k_ref, b_ref, c_ref, r_ref, tp, delta, parts):
    rows = t_ref.shape[0]
    base = pl.program_id(0) * rows

    @pl.when(pl.program_id(0) == 0)
    def _():
        lay_out(counts, b_ref, tp)
        solve_into(tp, x_ref, k_ref, delta, parts)

    c_ref[...] = jnp.zeros(c_ref.shape, jnp.float32)
    r_ref[...] = t_ref[...] - fitted(s_ref, parts)
    for q in range(SLOTS):
        row = own_row[q] - base

        @pl.when((row >= 0) & (row < rows))
        def _():
            got = delta[pl.ds(own_pos[q], 1), :]
            c_ref[pl.ds(row, 1), :] = got
            r_ref[pl.ds(row, 1), :] = r_ref[pl.ds(row, 1), :] - RIDGE * got


def slow_tail_kernel(idx_ref, t_ref, s_ref, x_ref, k_ref, tp_ref, c_ref, r_ref, delta, parts, exact):
    n, w = tp_ref.shape
    rows = t_ref.shape[0]

    @pl.when(pl.program_id(0) == 0)
    def _():
        solve_into(tp_ref, x_ref, k_ref, delta, parts)
        for i, part in enumerate(split3(delta[...])):
            exact[:, i * w : (i + 1) * w] = part

    row = lax.broadcasted_iota(jnp.int32, (rows, n), 0) + pl.program_id(0) * rows
    sel = (idx_ref[0:1, :] == row).astype(jnp.bfloat16)
    got = jnp.dot(sel, exact[...], preferred_element_type=jnp.float32)
    coefs = (got[:, :w] + got[:, w : 2 * w]) + got[:, 2 * w :]
    c_ref[...] = coefs
    r_ref[...] = t_ref[...] - fitted(s_ref, parts) - RIDGE * coefs


def prefix(mask, tri):
    total = jnp.zeros((mask.shape[0], 1), jnp.float32)
    out = []
    for b in range(mask.shape[1] // 128):
        part = mask[:, b * 128 : (b + 1) * 128]
        out.append(jnp.dot(part.astype(jnp.bfloat16), tri, preferred_element_type=jnp.float32) + total)
        total = total + jnp.sum(part, axis=1, keepdims=True)
    return jnp.concatenate(out, axis=1), total


def plan_kernel(me, b_ref, f_ref, t_ref, own_ref, list_ref, count_ref, p_ref, own_t_ref, *, shift, far, mid, near):
    xh, z, y = me[0], me[1], me[2]
    lanes = b_ref.shape[1]
    idx = jnp.concatenate([b_ref[0:1, :], b_ref[1:2, :]], axis=1)
    m = idx.shape[1]
    one = lambda c: jnp.where(c, 1.0, 0.0)
    owner = lax.shift_right_logical(idx, shift)
    row = (idx & ((1 << shift) - 1)).astype(jnp.float32)
    hi = owner // (mid * near)
    oz = (owner // near) % mid
    oy = owner % near
    group = hi * near + oy
    my_group = xh * near + y
    step = (lax.broadcasted_iota(jnp.int32, (1, m), 1) >= lanes).astype(jnp.int32)
    tri = one(
        lax.broadcasted_iota(jnp.int32, (128, 128), 0) < lax.broadcasted_iota(jnp.int32, (128, 128), 1)
    ).astype(jnp.bfloat16)
    mine = group == my_group
    masks = one((oz == lax.broadcasted_iota(jnp.int32, (mid, m), 0)) & mine)
    rank_all, _ = prefix(masks, tri)
    rank = jnp.sum(rank_all * masks, axis=0, keepdims=True)
    cls = one((step == lax.broadcasted_iota(jnp.int32, (8, m), 0)) & mine)
    crank_all, _ = prefix(cls, tri)
    crank = jnp.sum(crank_all * cls, axis=0, keepdims=True)
    own = mine & (oz == z)
    slot = lax.broadcasted_iota(jnp.int32, (SLOTS, m), 0).astype(jnp.float32)
    hit = own & (slot == rank)
    before = one(group < my_group)
    early = (step == 0).astype(jnp.float32)
    off0 = jnp.sum(before * early, axis=1, keepdims=True)
    off1 = jnp.sum(before * (1.0 - early), axis=1, keepdims=True)
    pos = jnp.where(step == 0, off0, off1 + float(lanes)) + crank
    take = lambda hits, v: jnp.sum(jnp.where(hits, v + 1.0, 0.0), axis=1, keepdims=True) - 1.0
    own_row = take(hit, row)
    column = lax.broadcasted_iota(jnp.int32, (SLOTS, 128), 1)
    both = jnp.where(column == 0, own_row, take(hit, pos))
    own_ref[...] = both.astype(jnp.int32)
    v = oz.astype(jnp.float32) * float(SLOTS) + rank
    v_shift = ((z - oz + mid) % mid).astype(jnp.float32) * float(SLOTS) + rank
    column = lax.broadcasted_iota(jnp.int32, (CAP, 128), 1)
    for s in range(2):
        half = slice(s * lanes, (s + 1) * lanes)
        u = lax.broadcasted_iota(jnp.int32, (CAP, lanes), 0).astype(jnp.float32)
        hits = mine[:, half] & (u == crank[:, half])
        both = jnp.where(column == 0, take(hits, v[:, half]), take(hits, v_shift[:, half]))
        list_ref[s * CAP : (s + 1) * CAP, :] = both.astype(jnp.int32)
    code = 2 * group + step
    classes = 2 * far * near
    count = jnp.sum(one(code == lax.broadcasted_iota(jnp.int32, (classes, m), 0)), axis=1, keepdims=True)
    owners = far * mid * near
    used = jnp.sum(one(owner == lax.broadcasted_iota(jnp.int32, (owners, m), 0)), axis=1, keepdims=True)
    over = one(jnp.max(used, axis=0, keepdims=True) > float(SLOTS)) + one(
        jnp.max(count, axis=0, keepdims=True) > float(CAP)
    )
    count_ref[0:classes, :] = jnp.broadcast_to(count, (classes, 128)).astype(jnp.int32)
    count_ref[classes:, :] = jnp.broadcast_to(over, (8, 128)).astype(jnp.int32)
    n = f_ref.shape[0]
    at = lax.broadcasted_iota(jnp.int32, (SLOTS, n), 1).astype(jnp.float32)
    sel = one(own_row == at).astype(jnp.bfloat16)
    hi, mid_part, low = (dot(sel, part) for part in split3(t_ref[...]))
    own_t_ref[...] = (hi + mid_part) + low
    own_p = dot(sel, f_ref[...]).astype(jnp.bfloat16)
    for i in range(mid):
        p_ref[i] = own_p


def pack_points_kernel(list_ref, b_ref, o_ref):
    shape = (list_ref.shape[0], b_ref.shape[0])
    sel = (list_ref[:, 0:1] == lax.broadcasted_iota(jnp.int32, shape, 1)).astype(jnp.bfloat16)
    packed = dot(sel, b_ref[...]).astype(jnp.bfloat16)
    for i in range(o_ref.shape[0]):
        o_ref[i] = packed


def pack_targets_kernel(list_ref, *refs):
    *b_refs, o_ref = refs
    b = jnp.concatenate([r[...] for r in b_refs], axis=0)
    shape = (list_ref.shape[0], b.shape[0])
    sel = (list_ref[:, 1:2] == lax.broadcasted_iota(jnp.int32, shape, 1)).astype(jnp.bfloat16)
    hi, mid, low = (dot(sel, part) for part in split3(b))
    packed = (hi + mid) + low
    for i in range(o_ref.shape[0]):
        o_ref[i] = packed


def full(shape):
    return pl.BlockSpec(shape, lambda i: (0,) * len(shape))


def tile(rows, width):
    return pl.BlockSpec((rows, width), lambda i: (i, 0))


def pick_points(idx_col, f):
    m, n, w = idx_col.shape[0], *f.shape
    bm = 64
    return pl.pallas_call(
        pick_points_kernel,
        grid=(m // bm,),
        in_specs=[tile(bm, 1), full((n, w))],
        out_specs=tile(bm, w),
        out_shape=jax.ShapeDtypeStruct((m, w), jnp.bfloat16),
        name="pick_points",
    )(idx_col, f)


def pick_targets(idx_col, t):
    m, n, w = idx_col.shape[0], *t.shape
    bm = 64
    return pl.pallas_call(
        pick_targets_kernel,
        grid=(m // bm,),
        in_specs=[tile(bm, 1), full((n, w))],
        out_specs=tile(bm, w),
        out_shape=jax.ShapeDtypeStruct((m, w), jnp.float32),
        scratch_shapes=[pltpu.VMEM((n, 3 * w), jnp.bfloat16)],
        name="pick_targets",
        cost_estimate=pl.CostEstimate(flops=6 * m * n * w, transcendentals=0, bytes_accessed=8 * n * w),
    )(idx_col, t)


def factor(points, own, width, blocked):
    m = points[0].shape[0]
    n = m // 2
    f32, half = jnp.float32, jnp.bfloat16
    vmem = pl.BlockSpec(memory_space=pltpu.VMEM)
    return pl.pallas_call(
        functools.partial(factor_kernel, width=width, blocked=blocked),
        out_shape=(
            jax.ShapeDtypeStruct((n, 2 * n), half),
            jax.ShapeDtypeStruct((2, n, 2 * n), half),
            jax.ShapeDtypeStruct((own[0].shape[0], 2 * m), half),
        ),
        in_specs=[vmem] * 8,
        out_specs=(vmem,) * 3,
        scratch_shapes=[
            pltpu.VMEM((2, n, n), f32),
            pltpu.VMEM((2, LEAF, n), f32),
            pltpu.VMEM((2, n, LEAF), f32),
            pltpu.VMEM((2, LEAF, LEAF), f32),
        ],
        name="factor",
        cost_estimate=pl.CostEstimate(flops=40 * 10**9, transcendentals=0, bytes_accessed=8 * m * m),
    )(*points, *own)


SMEM = pl.BlockSpec(memory_space=pltpu.SMEM)


def tail(counts, own_row, own_pos, t, slab, x, k, buffer):
    n, width = t.shape
    m = 2 * k.shape[0]
    bm = 256
    return pl.pallas_call(
        tail_kernel,
        grid=(n // bm,),
        in_specs=[SMEM, SMEM, SMEM, tile(bm, width), tile(bm, 2 * m), full(x.shape), full(k.shape), full(buffer.shape)],
        out_specs=(tile(bm, width), tile(bm, width)),
        out_shape=(jax.ShapeDtypeStruct(t.shape, jnp.float32),) * 2,
        scratch_shapes=[
            pltpu.VMEM((m + CAP + 8, width), jnp.float32),
            pltpu.VMEM((m, width), jnp.float32),
            pltpu.VMEM((m, 2 * width), jnp.bfloat16),
        ],
        name="tail",
    )(counts, own_row, own_pos, t, slab, x, k, buffer)


def slow_tail(idx_row, t, slab, x, k, tp):
    n, width = t.shape
    m = tp.shape[0]
    bm = 64
    return pl.pallas_call(
        slow_tail_kernel,
        grid=(n // bm,),
        in_specs=[full(idx_row.shape), tile(bm, width), tile(bm, 2 * m), full(x.shape), full(k.shape), full(tp.shape)],
        out_specs=(tile(bm, width), tile(bm, width)),
        out_shape=(jax.ShapeDtypeStruct(t.shape, jnp.float32),) * 2,
        scratch_shapes=[
            pltpu.VMEM((m, width), jnp.float32),
            pltpu.VMEM((m, 2 * width), jnp.bfloat16),
            pltpu.VMEM((m, 3 * width), jnp.bfloat16),
        ],
        name="slow_tail",
    )(idx_row, t, slab, x, k, tp)


def plan(me, block_index, f, t, sizes):
    far, mid, near = sizes
    n, w = f.shape
    vmem = pl.BlockSpec(memory_space=pltpu.VMEM)
    i32 = jnp.int32
    return pl.pallas_call(
        functools.partial(plan_kernel, shift=n.bit_length() - 1, far=far, mid=mid, near=near),
        in_specs=[SMEM, vmem, vmem, vmem],
        out_specs=(vmem,) * 5,
        out_shape=(
            jax.ShapeDtypeStruct((SLOTS, 128), i32),
            jax.ShapeDtypeStruct((2 * CAP, 128), i32),
            jax.ShapeDtypeStruct((2 * far * near + 8, 128), i32),
            jax.ShapeDtypeStruct((mid, SLOTS, w), f.dtype),
            jax.ShapeDtypeStruct((SLOTS, t.shape[1]), t.dtype),
        ),
        name="plan",
    )(me, block_index, f, t)


def pack(kernel, where, buffers, copies):
    m, w, dtype = where.shape[0], buffers[0].shape[1], buffers[0].dtype
    vmem = pl.BlockSpec(memory_space=pltpu.VMEM)
    return pl.pallas_call(
        kernel,
        in_specs=[vmem] * (1 + len(buffers)),
        out_specs=vmem,
        out_shape=jax.ShapeDtypeStruct((copies, m, w), dtype),
        name="pack",
    )(where, *buffers)


def dense_points(counts, buffer, m):
    w = buffer.shape[1]
    vmem = pl.BlockSpec(memory_space=pltpu.VMEM)
    return pl.pallas_call(
        dense_points_kernel,
        in_specs=[SMEM, vmem],
        out_specs=vmem,
        out_shape=jax.ShapeDtypeStruct((m, w), buffer.dtype),
        scratch_shapes=[pltpu.VMEM(buffer.shape, jnp.float32), pltpu.VMEM((m + CAP + 8, w), jnp.float32)],
        name="dense_points",
    )(counts, buffer)


def spread(copies, axes):
    parts = lax.all_to_all(copies, axes, split_axis=0, concat_axis=0, tiled=True)
    return parts.reshape(-1, copies.shape[2])


def exchange(parts):
    return lax.all_to_all(parts, ROWS, split_axis=0, concat_axis=0, tiled=True)


def scattered_sum(x, count):
    parts = exchange(x.reshape(count, x.shape[0] // count, x.shape[1]))
    return parts.sum(axis=0)


def gathered(x, count):
    parts = exchange(jnp.broadcast_to(x, (count, *x.shape)))
    return parts.reshape(-1, x.shape[1])


def over_cols(x):
    other = lax.ppermute(x, "xlo", SWAP)
    return (x, other, lax.ppermute(x, "core", SWAP), lax.ppermute(other, "core", SWAP))


def slow(features, targets, block_index):
    rows_here = features.shape[0]
    count = lax.axis_size(ROWS)
    width = features.shape[1] * lax.axis_size(COLS)
    idx = block_index.reshape(-1) - lax.axis_index(ROWS) * rows_here
    idx_col = idx[:, None]
    idx_row = jnp.broadcast_to(idx[None, :], (8, idx.shape[0]))
    own = over_cols(features)
    points = over_cols(gathered(scattered_sum(pick_points(idx_col, features), count), count))
    tp = gathered(scattered_sum(pick_targets(idx_col, targets), count), count)
    k, x, slab = factor(points, own, width, False)
    return tuple(slow_tail(idx_row, targets, slab, x, k, tp))


def shards(features, targets, block_index):
    width = features.shape[1] * lax.axis_size(COLS)
    sizes = tuple(lax.axis_size(a) for a in ROWS)
    me = jnp.stack([lax.axis_index(a) for a in ROWS]).astype(jnp.int32)
    across = (ROWS[0], ROWS[2])
    own_list, where, counts, p, t = plan(me, block_index, features, targets, sizes)
    own_row, own_pos = own_list[:, 0], own_list[:, 1]
    classes = counts.shape[0] - 8
    overflow = counts[classes, 0] > 0
    counts = counts[:classes, 0]
    copies = sizes[0] * sizes[2]
    other = lax.ppermute(features, "xlo", SWAP)
    p = spread(p, ROWS[1])
    p, other, t = lax.optimization_barrier((p, other, t))
    p = spread(pack(pack_points_kernel, where, [p], copies), across)
    turn = sizes[1]
    around = [t] + [lax.ppermute(t, ROWS[1], [(i, (i + k) % turn) for i in range(turn)]) for k in range(1, turn)]
    far = [lax.ppermute(x, "core", SWAP) for x in (features, other)]
    p, *far = lax.optimization_barrier((p, *far))
    own = (features, other, *far)
    p = dense_points(counts, p, block_index.size)
    later, _ = lax.optimization_barrier((where, p))
    t = pack(pack_targets_kernel, later, around, copies)
    mate = lax.ppermute(p, "xlo", SWAP)
    mate, t = lax.optimization_barrier((mate, t))
    t = spread(t, across)
    points = (p, mate, lax.ppermute(p, "core", SWAP), lax.ppermute(mate, "core", SWAP))
    k, x, slab = factor(points, own, width, True)
    return lax.cond(
        overflow,
        lambda: slow(features, targets, block_index),
        lambda: tuple(tail(counts, own_row, own_pos, targets, slab, x, k, t)),
    )


def solution(mesh):
    split = Mesh(mesh.devices.reshape(2, 8, 4, 2, 2), ROWS + COLS)
    return jax.shard_map(
        shards,
        mesh=split,
        in_specs=(P(ROWS, COLS), P(ROWS, COLS), P()),
        out_specs=(P(ROWS, COLS), P(ROWS, COLS)),
        check_vma=False,
    )
```

```python
import functools

import jax
import jax.numpy as jnp
from jax import lax
from jax.experimental import pallas as pl
from jax.experimental.pallas import tpu as pltpu
from jax.sharding import Mesh
from jax.sharding import PartitionSpec as P

ROWS = ("r0", "r1", "r2")
COLS = ("xlo", "core")
RIDGE = 1.0
LEAF = 128
SWAP = [(0, 1), (1, 0)]
SLOTS = 32
CAP = 96
SMEM = pl.BlockSpec(memory_space=pltpu.SMEM)


def LIMIT(mib):
    return pltpu.CompilerParams(vmem_limit_bytes=mib * 2**20)


def dot(a, b):
    return jnp.dot(a, b, preferred_element_type=jnp.float32)


def mm6(a, b):
    a0, a1, a2 = split3(a)
    b0, b1, b2 = split3(b)
    return dot(
        jnp.concatenate([a2, a1, a0, a1, a0, a0], axis=1),
        jnp.concatenate([b0, b1, b2, b0, b1, b0], axis=0),
    )


def mm_nt(a, b):
    return lax.dot_general(a, b, (((1,), (1,)), ((), ())), preferred_element_type=jnp.float32)


def inv2(a, b, d):
    i = 1.0 / (a * d - b * b)
    return d * i, -b * i, a * i


def leaf_inverse(m):
    n = m.shape[-1]
    lane = lax.broadcasted_iota(jnp.int32, (1, 1, n), 2)
    sub = lax.broadcasted_iota(jnp.int32, (1, n, 1), 1)
    for j in range(0, n, 4):
        c = [jnp.broadcast_to(m[:, :, j + q : j + q + 1], m.shape) for q in range(4)]
        e = lambda p, q: c[q][:, j + p : j + p + 1, :]
        r = []
        for q in range(4):
            row = m[:, j + q : j + q + 1, :]
            for w in range(4):
                row = jnp.where(lane == j + w, 1.0 if w == q else 0.0, row)
            r.append(row)
        x11, x12, x22 = inv2(e(0, 0), e(0, 1), e(1, 1))
        b = [[e(0, 2), e(0, 3)], [e(1, 2), e(1, 3)]]
        y = [
            [x11 * b[0][q] + x12 * b[1][q] for q in range(2)],
            [x12 * b[0][q] + x22 * b[1][q] for q in range(2)],
        ]
        s = lambda p, q, base: base - (b[0][p] * y[0][q] + b[1][p] * y[1][q])
        z11, z12, z22 = inv2(s(0, 0, e(2, 2)), s(0, 1, e(2, 3)), s(1, 1, e(3, 3)))
        w0 = x11 * r[0] + x12 * r[1]
        w1 = x12 * r[0] + x22 * r[1]
        t0 = r[2] - (b[0][0] * w0 + b[1][0] * w1)
        t1 = r[3] - (b[0][1] * w0 + b[1][1] * w1)
        s2 = z11 * t0 + z12 * t1
        s3 = z12 * t0 + z22 * t1
        s0 = w0 - (y[0][0] * s2 + y[0][1] * s3)
        s1 = w1 - (y[1][0] * s2 + y[1][1] * s3)
        new = jnp.where((lane >= j) & (lane < j + 4), 0.0, m)
        new = new - ((c[0] * s0 + c[1] * s1) + (c[2] * s2 + c[3] * s3))
        for q, sq in enumerate((s0, s1, s2, s3)):
            new = jnp.where(sub == j + q, sq, new)
        m = new
    return m


def invert_by_pivots(a_ref):
    n = a_ref.shape[-1]
    lane = lax.broadcasted_iota(jnp.int32, (1, 1, n), 2)
    strip = 64
    high = lax.broadcasted_iota(jnp.int32, (1, strip, 1), 1)

    def step(j, carry):
        r = a_ref[:, pl.ds(j, 1), :]
        ip = 1.0 / jnp.sum(jnp.where(lane == j, r, 0.0), axis=2, keepdims=True)
        r = jnp.where(lane == j, ip, r * ip)

        def rows(i, carry):
            here = pl.ds(pl.multiple_of(i * strip, strip), strip)
            x = a_ref[:, here, :]
            c = jnp.sum(jnp.where(lane == j, x, 0.0), axis=2, keepdims=True)
            x = jnp.where(lane == j, 0.0, x) - c * r
            a_ref[:, here, :] = jnp.where(high + i * strip == j, r, x)
            return carry

        return lax.fori_loop(0, n // strip, rows, carry)

    lax.fori_loop(0, n, step, 0)


def pick_points_kernel(idx_ref, f_ref, o_ref):
    n = f_ref.shape[0]
    sel = (idx_ref[...] == lax.broadcasted_iota(jnp.int32, (idx_ref.shape[0], n), 1)).astype(jnp.bfloat16)
    o_ref[...] = jnp.dot(sel, f_ref[...], preferred_element_type=jnp.float32).astype(jnp.bfloat16)


def split3(x):
    hi = x.astype(jnp.bfloat16)
    rest = x - hi.astype(jnp.float32)
    mid = rest.astype(jnp.bfloat16)
    low = (rest - mid.astype(jnp.float32)).astype(jnp.bfloat16)
    return hi, mid, low


def pick_targets_kernel(idx_ref, t_ref, o_ref, parts):
    n, w = t_ref.shape

    @pl.when(pl.program_id(0) == 0)
    def _():
        for i, part in enumerate(split3(t_ref[...])):
            parts[:, i * w : (i + 1) * w] = part

    sel = (idx_ref[...] == lax.broadcasted_iota(jnp.int32, (idx_ref.shape[0], n), 1)).astype(jnp.bfloat16)
    got = jnp.dot(sel, parts[...], preferred_element_type=jnp.float32)
    o_ref[...] = (got[:, :w] + got[:, w : 2 * w]) + got[:, 2 * w :]


def factor_kernel(p0, p1, p2, p3, f0, f1, f2, f3, k_ref, x_ref, s_ref, a_ref, r_ref, c_ref, d_ref, sq_ref, *, width, blocked):
    points, own = (p0, p1, p2, p3), (f0, f1, f2, f3)
    m = p0.shape[0]
    n = m // 2
    gram = lambda a, b: sum(mm_nt(p[a * n : (a + 1) * n, :], p[b * n : (b + 1) * n, :]) for p in points)
    eye = lax.broadcasted_iota(jnp.int32, (n, n), 0) == lax.broadcasted_iota(jnp.int32, (n, n), 1)
    scale = -(2.0 / width)
    rows, cols = [], []
    for s in range(2):
        g = gram(s, s)
        diag = jnp.where(eye, g, 0.0)
        rows.append(jnp.sum(diag, axis=0, keepdims=True))
        cols.append(jnp.sum(diag, axis=1, keepdims=True))
        k = jnp.exp(scale * (cols[s] + rows[s] - 2.0 * g))
        a_ref[s] = k + jnp.where(eye, RIDGE, 0.0)
    sq_ref[...] = jnp.broadcast_to(cols[1], sq_ref.shape)
    point_sq = jnp.concatenate(rows, axis=1)
    d_ref[...] = a_ref[:, 0:LEAF, 0:LEAF]
    c_ref[...] = jnp.zeros(c_ref.shape, jnp.float32)
    r_ref[...] = jnp.zeros(r_ref.shape, jnp.float32)
    blocks = n // LEAF
    tile_rows = f0.shape[0] // blocks

    def slab_tile(k):
        here = pl.ds(pl.multiple_of(k * tile_rows, tile_rows), tile_rows)
        g, sq = 0.0, 0.0
        for f, p in zip(own, points):
            x = f[here, :]
            g = g + mm_nt(x, p[...])
            xf = x.astype(jnp.float32)
            sq = sq + xf * xf
        slab = jnp.exp(scale * (jnp.sum(sq, axis=1, keepdims=True) + point_sq - 2.0 * g))
        s_ref[here, :m], s_ref[here, m:] = split2(slab)
        here = pl.ds(pl.multiple_of(k * LEAF, LEAF), LEAF)
        there = pl.ds(pl.multiple_of(n + k * LEAF, LEAF), LEAF)
        g = sum(mm_nt(p[there, :], p[0:n, :]) for p in points)
        k_ref[here, :n], k_ref[here, n:] = split2(jnp.exp(scale * (sq_ref[here, 0:1] + rows[0] - 2.0 * g)))

    def step(k, carry):
        block = lambda i: pl.ds(pl.multiple_of(i * LEAF, LEAF), LEAF)
        at, ahead, last = block(k), block(jnp.minimum(k + 1, blocks - 1)), block(jnp.maximum(k - 1, 0))
        if not blocked:
            slab_tile(k)
            return carry
        dinv = leaf_inverse(d_ref[...])
        for s in range(2):
            a_ref[s] = a_ref[s] - mm6(c_ref[s], r_ref[s])

        @pl.when(k > 0)
        def _():
            for s in range(2):
                a_ref[s, last, :] = r_ref[s]

        slab_tile(k)
        for s in range(2):
            r_ref[s] = mm6(dinv[s], a_ref[s, at, :])
            r_ref[s, :, at] = dinv[s]
            c_ref[s] = a_ref[s, :, at]
            a_ref[s, :, at] = jnp.zeros((n, LEAF), jnp.float32)
            d_ref[s] = a_ref[s, ahead, ahead] - mm6(c_ref[s, ahead, :], r_ref[s, :, ahead])
        return carry

    lax.fori_loop(0, blocks, step, 0)
    if not blocked:
        invert_by_pivots(a_ref)
        for s in range(2):
            x_ref[s, :, :n], x_ref[s, :, n:] = split2(a_ref[s])
        return
    for s in range(2):
        done = a_ref[s] - mm6(c_ref[s], r_ref[s])
        x_ref[s, :, :n], x_ref[s, :, n:] = split2(done)
        x_ref[s, n - LEAF : n, :n], x_ref[s, n - LEAF : n, n:] = split2(r_ref[s])


def split2(x):
    hi = x.astype(jnp.bfloat16)
    return hi, (x - hi.astype(jnp.float32)).astype(jnp.bfloat16)


def product3(a_pair, b):
    k = a_pair.shape[1] // 2
    hi, low = split2(b)
    both = dot(a_pair[:, :k], jnp.concatenate([hi, low], axis=1))
    return both[:, : b.shape[1]] + (both[:, b.shape[1] :] + dot(a_pair[:, k:], hi))


def solve_into(tp, x_ref, k_ref, delta, parts):
    n = x_ref.shape[1]
    w = delta.shape[1]
    first = product3(x_ref[0], tp[0:n, :])
    second = product3(x_ref[1], tp[n : 2 * n, :] - product3(k_ref[...], first))
    delta[0:n, :] = first
    delta[n : 2 * n, :] = second
    parts[0:n, :w], parts[0:n, w:] = split2(first)
    parts[n : 2 * n, :w], parts[n : 2 * n, w:] = split2(second)


def fitted(s_ref, parts):
    m, w = parts.shape[0], parts.shape[1] // 2
    both = jnp.dot(s_ref[:, :m], parts[...], preferred_element_type=jnp.float32)
    low = jnp.dot(s_ref[:, m:], parts[:, :w], preferred_element_type=jnp.float32)
    return both[:, :w] + (both[:, w:] + low)


def lay_out(counts, b_ref, dense):
    groups = counts.shape[0] // 2
    lanes = dense.shape[1]
    row = lax.broadcasted_iota(jnp.int32, (CAP + 8, lanes), 0)
    for s in range(2):
        at = jnp.int32(s * ((dense.shape[0] - CAP - 8) // 2))
        for g in range(groups):
            src = (2 * g + s) * CAP
            shift = at & 7
            window = pl.ds(pl.multiple_of(at - shift, 8), CAP + 8)
            x = jnp.concatenate([b_ref[src : src + CAP, :], b_ref[src : src + 8, :]], axis=0)
            dense[window, :] = jnp.where(row >= shift, pltpu.roll(x, shift, 0), dense[window, :])
            at = at + counts[2 * g + s]


def dense_points_kernel(counts, b_ref, o_ref, wide, dense):
    wide[...] = b_ref[...].astype(jnp.float32)

    lay_out(counts, wide, dense)
    o_ref[...] = dense[0 : o_ref.shape[0], :].astype(jnp.bfloat16)


def tail_kernel(counts, own_row, own_pos, t_ref, s_ref, x_ref, k_ref, b_ref, c_ref, r_ref, tp, delta, parts):
    rows = t_ref.shape[0]
    base = pl.program_id(0) * rows

    @pl.when(pl.program_id(0) == 0)
    def _():
        lay_out(counts, b_ref, tp)
        solve_into(tp, x_ref, k_ref, delta, parts)

    c_ref[...] = jnp.zeros(c_ref.shape, jnp.float32)
    r_ref[...] = t_ref[...] - fitted(s_ref, parts)
    for q in range(SLOTS):
        row = own_row[q] - base

        @pl.when((row >= 0) & (row < rows))
        def _():
            got = delta[pl.ds(own_pos[q], 1), :]
            c_ref[pl.ds(row, 1), :] = got
            r_ref[pl.ds(row, 1), :] = r_ref[pl.ds(row, 1), :] - RIDGE * got


def slow_tail_kernel(idx_ref, t_ref, s_ref, x_ref, k_ref, tp_ref, c_ref, r_ref, delta, parts, exact):
    n, w = tp_ref.shape
    rows = t_ref.shape[0]

    @pl.when(pl.program_id(0) == 0)
    def _():
        solve_into(tp_ref, x_ref, k_ref, delta, parts)
        for i, part in enumerate(split3(delta[...])):
            exact[:, i * w : (i + 1) * w] = part

    row = lax.broadcasted_iota(jnp.int32, (rows, n), 0) + pl.program_id(0) * rows
    sel = (idx_ref[0:1, :] == row).astype(jnp.bfloat16)
    got = jnp.dot(sel, exact[...], preferred_element_type=jnp.float32)
    coefs = (got[:, :w] + got[:, w : 2 * w]) + got[:, 2 * w :]
    c_ref[...] = coefs
    r_ref[...] = t_ref[...] - fitted(s_ref, parts) - RIDGE * coefs


def prefix(mask, tri):
    total = jnp.zeros((mask.shape[0], 1), jnp.float32)
    out = []
    for b in range(mask.shape[1] // 128):
        part = mask[:, b * 128 : (b + 1) * 128]
        out.append(jnp.dot(part.astype(jnp.bfloat16), tri, preferred_element_type=jnp.float32) + total)
        total = total + jnp.sum(part, axis=1, keepdims=True)
    return jnp.concatenate(out, axis=1), total


def plan_kernel(me, b_ref, f_ref, own_ref, list_ref, count_ref, p_ref, *, shift, far, mid, near):
    xh, z, y = me[0], me[1], me[2]
    lanes = b_ref.shape[1]
    idx = jnp.concatenate([b_ref[0:1, :], b_ref[1:2, :]], axis=1)
    m = idx.shape[1]
    one = lambda c: jnp.where(c, 1.0, 0.0)
    owner = lax.shift_right_logical(idx, shift)
    row = (idx & ((1 << shift) - 1)).astype(jnp.float32)
    hi = owner // (mid * near)
    oz = (owner // near) % mid
    oy = owner % near
    group = hi * near + oy
    my_group = xh * near + y
    step = (lax.broadcasted_iota(jnp.int32, (1, m), 1) >= lanes).astype(jnp.int32)
    tri = one(
        lax.broadcasted_iota(jnp.int32, (128, 128), 0) < lax.broadcasted_iota(jnp.int32, (128, 128), 1)
    ).astype(jnp.bfloat16)
    mine = group == my_group
    masks = one((oz == lax.broadcasted_iota(jnp.int32, (mid, m), 0)) & mine)
    rank_all, _ = prefix(masks, tri)
    rank = jnp.sum(rank_all * masks, axis=0, keepdims=True)
    cls = one((step == lax.broadcasted_iota(jnp.int32, (8, m), 0)) & mine)
    crank_all, _ = prefix(cls, tri)
    crank = jnp.sum(crank_all * cls, axis=0, keepdims=True)
    own = mine & (oz == z)
    slot = lax.broadcasted_iota(jnp.int32, (SLOTS, m), 0).astype(jnp.float32)
    hit = own & (slot == rank)
    before = one(group < my_group)
    early = (step == 0).astype(jnp.float32)
    off0 = jnp.sum(before * early, axis=1, keepdims=True)
    off1 = jnp.sum(before * (1.0 - early), axis=1, keepdims=True)
    pos = jnp.where(step == 0, off0, off1 + float(lanes)) + crank
    take = lambda hits, v: jnp.sum(jnp.where(hits, v + 1.0, 0.0), axis=1, keepdims=True) - 1.0
    own_row = take(hit, row)
    column = lax.broadcasted_iota(jnp.int32, (SLOTS, 128), 1)
    both = jnp.where(column == 0, own_row, take(hit, pos))
    own_ref[...] = both.astype(jnp.int32)
    v = oz.astype(jnp.float32) * float(SLOTS) + rank
    v_shift = ((z - oz + mid) % mid).astype(jnp.float32) * float(SLOTS) + rank
    column = lax.broadcasted_iota(jnp.int32, (CAP, 128), 1)
    for s in range(2):
        half = slice(s * lanes, (s + 1) * lanes)
        u = lax.broadcasted_iota(jnp.int32, (CAP, lanes), 0).astype(jnp.float32)
        hits = mine[:, half] & (u == crank[:, half])
        both = jnp.where(column == 0, take(hits, v[:, half]), take(hits, v_shift[:, half]))
        list_ref[s * CAP : (s + 1) * CAP, :] = both.astype(jnp.int32)
    code = 2 * group + step
    classes = 2 * far * near
    count = jnp.sum(one(code == lax.broadcasted_iota(jnp.int32, (classes, m), 0)), axis=1, keepdims=True)
    owners = far * mid * near
    used = jnp.sum(one(owner == lax.broadcasted_iota(jnp.int32, (owners, m), 0)), axis=1, keepdims=True)
    over = one(jnp.max(used, axis=0, keepdims=True) > float(SLOTS)) + one(
        jnp.max(count, axis=0, keepdims=True) > float(CAP)
    )
    count_ref[0:classes, :] = jnp.broadcast_to(count, (classes, 128)).astype(jnp.int32)
    count_ref[classes:, :] = jnp.broadcast_to(over, (8, 128)).astype(jnp.int32)
    n = f_ref.shape[0]
    at = lax.broadcasted_iota(jnp.int32, (SLOTS, n), 1).astype(jnp.float32)
    sel = one(own_row == at).astype(jnp.bfloat16)
    own_p = dot(sel, f_ref[...]).astype(jnp.bfloat16)
    for i in range(mid):
        p_ref[i] = own_p


def own_targets_kernel(own_row, t_ref, o_ref):
    for q in range(SLOTS):
        row = own_row[q]
        got = t_ref[pl.ds(jnp.maximum(row, 0), 1), :]
        o_ref[q : q + 1, :] = jnp.where(row >= 0, got, 0.0)


def pack_points_kernel(list_ref, b_ref, o_ref):
    shape = (list_ref.shape[0], b_ref.shape[0])
    sel = (list_ref[:, 0:1] == lax.broadcasted_iota(jnp.int32, shape, 1)).astype(jnp.bfloat16)
    packed = dot(sel, b_ref[...]).astype(jnp.bfloat16)
    for i in range(o_ref.shape[0]):
        o_ref[i] = packed


def pack_targets_kernel(list_ref, *refs):
    *b_refs, o_ref = refs
    b = jnp.concatenate([r[...] for r in b_refs], axis=0)
    shape = (list_ref.shape[0], b.shape[0])
    sel = (list_ref[:, 1:2] == lax.broadcasted_iota(jnp.int32, shape, 1)).astype(jnp.bfloat16)
    hi, mid, low = (dot(sel, part) for part in split3(b))
    packed = (hi + mid) + low
    for i in range(o_ref.shape[0]):
        o_ref[i] = packed


def full(shape):
    return pl.BlockSpec(shape, lambda i: (0,) * len(shape))


def tile(rows, width):
    return pl.BlockSpec((rows, width), lambda i: (i, 0))


def pick_points(idx_col, f):
    m, n, w = idx_col.shape[0], *f.shape
    bm = 64
    return pl.pallas_call(
        pick_points_kernel,
        grid=(m // bm,),
        in_specs=[tile(bm, 1), full((n, w))],
        out_specs=tile(bm, w),
        out_shape=jax.ShapeDtypeStruct((m, w), jnp.bfloat16),
        name="pick_points",
    )(idx_col, f)


def pick_targets(idx_col, t):
    m, n, w = idx_col.shape[0], *t.shape
    bm = 64
    return pl.pallas_call(
        pick_targets_kernel,
        grid=(m // bm,),
        in_specs=[tile(bm, 1), full((n, w))],
        out_specs=tile(bm, w),
        out_shape=jax.ShapeDtypeStruct((m, w), jnp.float32),
        scratch_shapes=[pltpu.VMEM((n, 3 * w), jnp.bfloat16)],
        name="pick_targets",
        cost_estimate=pl.CostEstimate(flops=6 * m * n * w, transcendentals=0, bytes_accessed=8 * n * w),
    )(idx_col, t)


def factor(points, own, width, blocked):
    m = points[0].shape[0]
    n = m // 2
    f32, half = jnp.float32, jnp.bfloat16
    vmem = pl.BlockSpec(memory_space=pltpu.VMEM)
    return pl.pallas_call(
        functools.partial(factor_kernel, width=width, blocked=blocked),
        out_shape=(
            jax.ShapeDtypeStruct((n, 2 * n), half),
            jax.ShapeDtypeStruct((2, n, 2 * n), half),
            jax.ShapeDtypeStruct((own[0].shape[0], 2 * m), half),
        ),
        in_specs=[vmem] * 8,
        out_specs=(vmem,) * 3,
        scratch_shapes=[
            pltpu.VMEM((2, n, n), f32),
            pltpu.VMEM((2, LEAF, n), f32),
            pltpu.VMEM((2, n, LEAF), f32),
            pltpu.VMEM((2, LEAF, LEAF), f32),
            pltpu.VMEM((n, 128), f32),
        ],
        compiler_params=LIMIT(30),
        name="factor",
        cost_estimate=pl.CostEstimate(flops=40 * 10**9, transcendentals=0, bytes_accessed=8 * m * m),
    )(*points, *own)


def tail(counts, own_row, own_pos, t, slab, x, k, buffer):
    n, width = t.shape
    m = 2 * k.shape[0]
    bm = 256
    return pl.pallas_call(
        tail_kernel,
        grid=(n // bm,),
        in_specs=[SMEM, SMEM, SMEM, tile(bm, width), tile(bm, 2 * m), full(x.shape), full(k.shape), full(buffer.shape)],
        out_specs=(tile(bm, width), tile(bm, width)),
        out_shape=(jax.ShapeDtypeStruct(t.shape, jnp.float32),) * 2,
        scratch_shapes=[
            pltpu.VMEM((m + CAP + 8, width), jnp.float32),
            pltpu.VMEM((m, width), jnp.float32),
            pltpu.VMEM((m, 2 * width), jnp.bfloat16),
        ],
        compiler_params=LIMIT(34),
        name="tail",
    )(counts, own_row, own_pos, t, slab, x, k, buffer)


def slow_tail(idx_row, t, slab, x, k, tp):
    n, width = t.shape
    m = tp.shape[0]
    bm = 64
    return pl.pallas_call(
        slow_tail_kernel,
        grid=(n // bm,),
        in_specs=[full(idx_row.shape), tile(bm, width), tile(bm, 2 * m), full(x.shape), full(k.shape), full(tp.shape)],
        out_specs=(tile(bm, width), tile(bm, width)),
        out_shape=(jax.ShapeDtypeStruct(t.shape, jnp.float32),) * 2,
        scratch_shapes=[
            pltpu.VMEM((m, width), jnp.float32),
            pltpu.VMEM((m, 2 * width), jnp.bfloat16),
            pltpu.VMEM((m, 3 * width), jnp.bfloat16),
        ],
        name="slow_tail",
    )(idx_row, t, slab, x, k, tp)


def plan(me, block_index, f, sizes):
    far, mid, near = sizes
    n, w = f.shape
    vmem = pl.BlockSpec(memory_space=pltpu.VMEM)
    i32 = jnp.int32
    return pl.pallas_call(
        functools.partial(plan_kernel, shift=n.bit_length() - 1, far=far, mid=mid, near=near),
        in_specs=[SMEM, vmem, vmem],
        out_specs=(vmem,) * 4,
        out_shape=(
            jax.ShapeDtypeStruct((SLOTS, 128), i32),
            jax.ShapeDtypeStruct((2 * CAP, 128), i32),
            jax.ShapeDtypeStruct((2 * far * near + 8, 128), i32),
            jax.ShapeDtypeStruct((mid, SLOTS, w), f.dtype),
        ),
        compiler_params=LIMIT(8),
        name="plan",
    )(me, block_index, f)


def own_targets(own_row, t):
    vmem = pl.BlockSpec(memory_space=pltpu.VMEM)
    return pl.pallas_call(
        own_targets_kernel,
        in_specs=[SMEM, vmem],
        out_specs=vmem,
        out_shape=jax.ShapeDtypeStruct((SLOTS, t.shape[1]), t.dtype),
        compiler_params=LIMIT(8),
        name="own_targets",
    )(own_row, t)


def pack(kernel, where, buffers, copies):
    m, w, dtype = where.shape[0], buffers[0].shape[1], buffers[0].dtype
    vmem = pl.BlockSpec(memory_space=pltpu.VMEM)
    return pl.pallas_call(
        kernel,
        in_specs=[vmem] * (1 + len(buffers)),
        out_specs=vmem,
        out_shape=jax.ShapeDtypeStruct((copies, m, w), dtype),
        compiler_params=LIMIT(12),
        name="pack",
    )(where, *buffers)


def dense_points(counts, buffer, m):
    w = buffer.shape[1]
    vmem = pl.BlockSpec(memory_space=pltpu.VMEM)
    return pl.pallas_call(
        dense_points_kernel,
        in_specs=[SMEM, vmem],
        out_specs=vmem,
        out_shape=jax.ShapeDtypeStruct((m, w), buffer.dtype),
        scratch_shapes=[pltpu.VMEM(buffer.shape, jnp.float32), pltpu.VMEM((m + CAP + 8, w), jnp.float32)],
        compiler_params=LIMIT(10),
        name="dense_points",
    )(counts, buffer)


def spread(copies, axes):
    parts = lax.all_to_all(copies, axes, split_axis=0, concat_axis=0, tiled=True)
    return parts.reshape(-1, copies.shape[2])


def exchange(parts):
    return lax.all_to_all(parts, ROWS, split_axis=0, concat_axis=0, tiled=True)


def scattered_sum(x, count):
    parts = exchange(x.reshape(count, x.shape[0] // count, x.shape[1]))
    return parts.sum(axis=0)


def gathered(x, count):
    parts = exchange(jnp.broadcast_to(x, (count, *x.shape)))
    return parts.reshape(-1, x.shape[1])


def over_cols(x):
    other = lax.ppermute(x, "xlo", SWAP)
    return (x, other, lax.ppermute(x, "core", SWAP), lax.ppermute(other, "core", SWAP))


def slow(features, targets, block_index):
    rows_here = features.shape[0]
    count = lax.axis_size(ROWS)
    width = features.shape[1] * lax.axis_size(COLS)
    idx = block_index.reshape(-1) - lax.axis_index(ROWS) * rows_here
    idx_col = idx[:, None]
    idx_row = jnp.broadcast_to(idx[None, :], (8, idx.shape[0]))
    own = over_cols(features)
    w = features.shape[1]
    rows = jnp.concatenate([pick_points(idx_col, features).astype(jnp.float32), pick_targets(idx_col, targets)], axis=1)
    rows = gathered(scattered_sum(rows, count), count)
    points = over_cols(rows[:, :w].astype(jnp.bfloat16))
    tp = rows[:, w:]
    k, x, slab = factor(points, own, width, False)
    return tuple(slow_tail(idx_row, targets, slab, x, k, tp))


def shards(features, targets, block_index):
    width = features.shape[1] * lax.axis_size(COLS)
    sizes = tuple(lax.axis_size(a) for a in ROWS)
    me = jnp.stack([lax.axis_index(a) for a in ROWS]).astype(jnp.int32)
    across = (ROWS[0], ROWS[2])
    own_list, where, counts, p = plan(me, block_index, features, sizes)
    own_row, own_pos = own_list[:, 0], own_list[:, 1]
    t = own_targets(own_row, targets)
    classes = counts.shape[0] - 8
    overflow = counts[classes, 0] > 0
    counts = counts[:classes, 0]
    copies = sizes[0] * sizes[2]
    other = lax.ppermute(features, "xlo", SWAP)
    p = spread(p, ROWS[1])
    p, other, t = lax.optimization_barrier((p, other, t))
    p = spread(pack(pack_points_kernel, where, [p], copies), across)
    turn = sizes[1]
    around = [t] + [lax.ppermute(t, ROWS[1], [(i, (i + k) % turn) for i in range(turn)]) for k in range(1, turn)]
    far = [lax.ppermute(x, "core", SWAP) for x in (features, other)]
    p, *far = lax.optimization_barrier((p, *far))
    own = (features, other, *far)
    p = dense_points(counts, p, block_index.size)
    later, _ = lax.optimization_barrier((where, p))
    t = pack(pack_targets_kernel, later, around, copies)
    mate = lax.ppermute(p, "xlo", SWAP)
    mate, t = lax.optimization_barrier((mate, t))
    t = spread(t, across)
    points = (p, mate, lax.ppermute(p, "core", SWAP), lax.ppermute(mate, "core", SWAP))
    k, x, slab = factor(points, own, width, True)
    return lax.cond(
        overflow,
        lambda: slow(features, targets, block_index),
        lambda: tuple(tail(counts, own_row, own_pos, targets, slab, x, k, t)),
    )


def solution(mesh):
    split = Mesh(mesh.devices.reshape(2, 8, 4, 2, 2), ROWS + COLS)
    return jax.shard_map(
        shards,
        mesh=split,
        in_specs=(P(ROWS, COLS), P(ROWS, COLS), P()),
        out_specs=(P(ROWS, COLS), P(ROWS, COLS)),
        check_vma=False,
    )
```
